32 devices in a mesh: dp: 16 (over z, y, x), mp: 2 (over core).
Axes of the slice: x: 2, y: 2, z: 4, core: 2. Of those that a mesh axis runs over, the one named last changes fastest.
Arguments:
- tokens: bfloat16 [8192, 768], P('dp'), may hold values from -6 to 6
- lengths: int32 [16], P('dp'), may hold values from 40 to 512, as said below
- cotangent: bfloat16 [8192, 768], P('dp'), may hold values from -6 to 6
- query_weight: bfloat16 [768, 768], P(None, 'mp'), may hold values from -0.21875 to 0.21875
- query_bias: bfloat16 [768], P('mp'), may hold values from -3 to 3
- key_weight: bfloat16 [768, 768], P(None, 'mp'), may hold values from -0.21875 to 0.21875
- value_weight: bfloat16 [768, 768], P(None, 'mp'), may hold values from -0.21875 to 0.21875
- value_bias: bfloat16 [768], P('mp'), may hold values from -1 to 1
- out_weight: bfloat16 [768, 768], P('mp'), may hold values from -1.75 to 1.75
- out_bias: bfloat16 [768], replicated, may hold values from -3 to 3
- mid_gain: bfloat16 [768], replicated, may hold values from 0.5 to 1.5
- mid_shift: bfloat16 [768], replicated, may hold values from -3 to 3
- up_weight: bfloat16 [768, 3072], P(None, 'mp'), may hold values from -0.21875 to 0.21875
- up_bias: bfloat16 [3072], P('mp'), may hold values from -3 to 3
- down_weight: bfloat16 [3072, 768], P('mp'), may hold values from -0.15625 to 0.15625
- down_bias: bfloat16 [768], replicated, may hold values from -3 to 3
- final_gain: bfloat16 [768], replicated, may hold values from 0.5 to 1.5
- final_shift: bfloat16 [768], replicated, may hold values from -3 to 3
Outputs:
- layer_out: bfloat16 [8192, 768], P('dp')
- input_grad: bfloat16 [8192, 768], P('dp')
- query_weight_grad: float32 [768, 768], P(None, 'mp')
- query_bias_grad: float32 [768], P('mp')
- key_weight_grad: float32 [768, 768], P(None, 'mp')
- value_weight_grad: float32 [768, 768], P(None, 'mp')
- value_bias_grad: float32 [768], P('mp')
- out_weight_grad: float32 [768, 768], P('mp')
- out_bias_grad: float32 [768], replicated
- mid_gain_grad: float32 [768], replicated
- mid_shift_grad: float32 [768], replicated
- up_weight_grad: float32 [768, 3072], P(None, 'mp')
- up_bias_grad: float32 [3072], P('mp')
- down_weight_grad: float32 [3072, 768], P('mp')
- down_bias_grad: float32 [768], replicated
- final_gain_grad: float32 [768], replicated
- final_shift_grad: float32 [768], replicated
The draws below stay inside these ranges and needn't reach their ends.
Inputs may be any that keep to these rules, and one draw needn't show every extreme that they name: `lengths`: real tokens of each page; key slots at or beyond it are padding. Some page has exactly 512 and some exactly 40.
All inputs are finite; a program needn't handle non-finite values.
Results may differ from the reference program's by a relative error of at most 0.015.
The reference program's roundings to bfloat16 on the way count: a program that leaves them out, or rounds other values in their place, can miss the bound.
Values sent between devices are 32-bit elements; how exact they have to be, the bound alone decides.
No kernel may reach another device: no remote copies, remote signals or barrier semaphores. Data moves between devices by JAX's collectives and lax.ppermute only.
A program may use at most 128 MiB of HBM per device.

```python
import jax
import jax.numpy as jnp
from jax import lax

D = 768
DH = 64
FF = 3072
SEQ = 512
MIN_LEN = 40
PAGES = 16
TOKENS = 8192


def draw_lengths(key, part):
    drawn = jax.random.randint(key, (PAGES,), MIN_LEN, SEQ + 1, dtype=jnp.int32)
    places = lax.iota(jnp.int32, PAGES)
    drawn = jnp.where(places == 0, SEQ, drawn)
    drawn = jnp.where(places == 1, MIN_LEN, drawn)
    return drawn.astype(jnp.int32)


def raised(values, rng, source, target, parts, factor):
    owner, partner = [(jnp.arange(values.shape[dim]) // (values.shape[dim] // parts)).reshape([-1 if axis == dim else 1 for axis in range(values.ndim)]) for dim in (source, target)]
    chosen = jax.random.permutation(rng, parts)[partner]
    strong = (owner == chosen) | (owner == (partner + parts // 2) % parts)
    return jnp.where(strong, factor * values, values)


def shard_levels(stream_key, dims, pieces, low, high):
    def one(position, blocks):
        steps = jax.random.uniform(jax.random.fold_in(jax.random.fold_in(stream_key, 6), position), (blocks,), jnp.float32, low / len(pieces), high / len(pieces))
        return jnp.repeat(jnp.exp(steps), dims[position] // blocks).reshape((-1,) + (1,) * (len(dims) - position - 1))

    level = one(*pieces[0])
    for cut in pieces[1:]:
        level = level * one(*cut)
    return level


def bell_draw(own_key, dims, deviation, limit, split=(), kind=jnp.bfloat16):
    array = jax.random.normal(own_key, dims, jnp.float32) * deviation
    if len(split) > 0:
        array = shard_levels(own_key, dims, split, -0.22, 0.18) * array
    return jnp.clip(array, min=-limit, max=limit).astype(kind)


def gaussian_with(key, extent, width, reach, split, heavy, held_as=jnp.bfloat16):
    values = width * jax.random.normal(key, extent, jnp.float32)
    if split:
        values = values * shard_levels(key, extent, split, -0.22, 0.18)
    return jnp.clip(raised(values, jax.random.fold_in(key, 3), *heavy), -reach, reach).astype(held_as)


def setup_inputs(seed: int = 0) -> dict:
    key_list = jax.random.split(jax.random.key(seed), 19)
    return {
        "tokens": gaussian_with(key_list[0], (TOKENS, D), 1.0, 6.0, ((0, 16),), (0, 1, 16, 2.0)),
        "lengths": draw_lengths(jax.random.fold_in(key_list[18], 71), 0),
        "cotangent": bell_draw(key_list[2], (TOKENS, D), 1.0, 6.0, ((0, 16),)),
        "query_weight": bell_draw(key_list[3], (D, D), D ** -0.5, 0.21875, ((1, 2),)),
        "query_bias": bell_draw(key_list[4], (D,), 0.5, 3.0, ((0, 2),)),
        "key_weight": bell_draw(key_list[5], (D, D), D ** -0.5, 0.21875, ((1, 2),)),
        "value_weight": bell_draw(key_list[6], (D, D), D ** -0.5, 0.21875, ((1, 2),)),
        "value_bias": bell_draw(key_list[7], (D,), 0.15, 1.0, ((0, 2),)),
        "out_weight": bell_draw(key_list[8], (D, D), (D // 64) ** -0.5, 1.75, ((0, 2),)),
        "out_bias": bell_draw(key_list[9], (D,), 0.5, 3.0),
        "mid_gain": jnp.clip(1.0 + 0.1 * jax.random.normal(key_list[10], (D,), jnp.float32), 0.5, 1.5).astype(jnp.bfloat16),
        "mid_shift": bell_draw(key_list[11], (D,), 0.5, 3.0),
        "up_weight": bell_draw(key_list[12], (D, FF), D ** -0.5, 0.21875, ((1, 2),)),
        "up_bias": bell_draw(key_list[13], (FF,), 0.5, 3.0, ((0, 2),)),
        "down_weight": bell_draw(key_list[14], (FF, D), (FF // 2) ** -0.5, 0.15625, ((0, 2),)),
        "down_bias": bell_draw(key_list[15], (D,), 0.5, 3.0),
        "final_gain": jnp.clip(1.0 + 0.1 * jax.random.normal(key_list[16], (D,), jnp.float32), 0.5, 1.5).astype(jnp.bfloat16),
        "final_shift": bell_draw(key_list[17], (D,), 0.5, 3.0),
    }


@jax.custom_vjp
def low(v):
    return lax.optimization_barrier(v.astype(jnp.bfloat16)).astype(jnp.float32)

@jax.custom_vjp
def low_back(v):
    return v

def low_keep(v):
    return (low(v), None)

def low_pass(kept, grad):
    return (grad,)

def back_keep(v):
    return (v, None)

def back_low(kept, grad):
    return (low(grad),)
low.defvjp(low_keep, low_pass)
low_back.defvjp(back_keep, back_low)
highest = lax.Precision.HIGHEST
norm_eps = 1e-12
score_scale = 0.125

def product(left, right):
    return jnp.dot(left, right, precision=highest)

def layer_norm(value, gain, shift):
    center = value - lax.optimization_barrier(jnp.mean(value, axis=-1, keepdims=True))
    spread = lax.optimization_barrier(jnp.mean(center * center, axis=-1, keepdims=True))
    return center * lax.rsqrt(spread + norm_eps) * gain + shift

def forward(inputs, page_lens, params):
    query_weight, query_bias, key_weight, value_weight, value_bias, out_weight, out_bias, mid_gain, mid_shift, up_weight, up_bias, down_weight, down_bias, final_gain, final_shift = params
    pages = page_lens.shape[0]
    length = inputs.shape[0] // pages
    heads = query_weight.shape[1] // DH
    query = low(low_back(product(inputs, query_weight) + query_bias)).reshape(pages, length, heads, DH)
    keys = low(low_back(product(inputs, key_weight))).reshape(pages, length, heads, DH)
    values = low(low_back(product(inputs, value_weight) + value_bias)).reshape(pages, length, heads, DH)
    scores = low_back(jnp.einsum('pqhd,pkhd->phqk', query, keys, precision=highest) * score_scale)
    visible = lax.iota(jnp.int32, length)[None, :] < page_lens.astype(jnp.int32)[:, None]
    scores = jnp.where(visible[:, None, None, :], scores, -1e+30)
    chances = low(low_back(jax.nn.softmax(scores, axis=-1)))
    context = jnp.einsum('phqk,pkhd->pqhd', chances, values, precision=highest)
    context = low(low_back(context.reshape(inputs.shape[0], heads * DH)))
    branch = low_back(product(context, out_weight))
    middle = layer_norm(inputs + branch + out_bias, mid_gain, mid_shift)
    before = low_back(product(low(middle), up_weight) + up_bias)
    active = low(jax.nn.gelu(before, approximate=False))
    down = low_back(product(active, down_weight))
    return layer_norm(middle + down + down_bias, final_gain, final_shift)

def reference(tokens, lengths, cotangent, query_weight, query_bias, key_weight, value_weight, value_bias, out_weight, out_bias, mid_gain, mid_shift, up_weight, up_bias, down_weight, down_bias, final_gain, final_shift):
    params = tuple((weight.astype(jnp.float32) for weight in (query_weight, query_bias, key_weight, value_weight, value_bias, out_weight, out_bias, mid_gain, mid_shift, up_weight, up_bias, down_weight, down_bias, final_gain, final_shift)))
    group = 8
    count = PAGES // group
    inputs = tokens.astype(jnp.float32).reshape(count, group * SEQ, D)
    upstream = cotangent.astype(jnp.float32).reshape(count, group * SEQ, D)
    page_lens = lengths.reshape(count, group)

    def visit(totals, item):
        block_in, block_lens, block_grad = item

        def local(block, *weights):
            return forward(block, block_lens, weights)
        result, pull = jax.vjp(local, block_in, *params)
        pulled = pull(block_grad)
        totals = tuple((total + grad for total, grad in zip(totals, pulled[1:])))
        return (totals, (result.astype(jnp.bfloat16), pulled[0].astype(jnp.bfloat16)))
    start = tuple((jnp.zeros_like(weight) for weight in params))
    totals, outputs = lax.scan(visit, start, (inputs, page_lens, upstream))
    layer_out = outputs[0].reshape(TOKENS, D)
    input_grad = outputs[1].reshape(TOKENS, D)
    return (layer_out, input_grad, totals[0], totals[1], totals[2], totals[3], totals[4], totals[5], totals[6], totals[7], totals[8], totals[9], totals[10], totals[11], totals[12], totals[13], totals[14])
```

```python
import functools

import jax
import jax.numpy as jnp
from jax import lax
from jax.experimental import pallas as pl
from jax.experimental.pallas import tpu as pltpu
from jax.sharding import PartitionSpec as P

DH = 64


norm_eps = 1e-12
score_scale = 0.125
root_half = 0.7071067811865476
inv_root_two_pi = 0.3989422804014327


def matmul(left, right):
    return jnp.dot(left, right, preferred_element_type=jnp.float32)


def matmul_flip(left, right):
    return lax.dot_general(
        left, right, (((1,), (1,)), ((), ())), preferred_element_type=jnp.float32
    )


def outer_sum(left, right):
    return lax.dot_general(
        left, right, (((0,), (0,)), ((), ())), preferred_element_type=jnp.float32
    )


def norm_forward(value, gain, shift):
    center = value - jnp.mean(value, axis=-1, keepdims=True)
    scale = lax.rsqrt(jnp.mean(center * center, axis=-1, keepdims=True) + norm_eps)
    normal = center * scale
    return (normal * gain.astype(jnp.float32) + shift.astype(jnp.float32), normal, scale)


def norm_backward(upper, normal, scale, gain):
    along = upper * gain.astype(jnp.float32)
    lower = scale * (
        along
        - jnp.mean(along, axis=-1, keepdims=True)
        - normal * jnp.mean(along * normal, axis=-1, keepdims=True)
    )
    return (lower, jnp.sum(upper * normal, axis=0), jnp.sum(upper, axis=0))


def masked_scores(query, keys, limit):
    scores = (
        jnp.einsum("qhd,khd->hqk", query, keys, preferred_element_type=jnp.float32) * score_scale
    )
    visible = lax.iota(jnp.int32, keys.shape[0]) < limit
    return jnp.where(visible[None, None, :], scores, -1e30)


def attend_page(item):
    query, keys, values, limit = item
    scores = masked_scores(query, keys, limit)
    top = jnp.max(scores, axis=-1, keepdims=True)
    raised = jnp.exp(scores - top)
    total = jnp.sum(raised, axis=-1, keepdims=True)
    chances = (raised / total).astype(jnp.bfloat16)
    context = jnp.einsum("hqk,khd->qhd", chances, values, preferred_element_type=jnp.float32)
    return (context.astype(jnp.bfloat16), top + jnp.log(total))


def attend_back(item):
    query, keys, values, limit, log_total, upstream = item
    chances = jnp.exp(masked_scores(query, keys, limit) - log_total)
    rounded = chances.astype(jnp.bfloat16)
    value_grad = jnp.einsum("hqk,qhd->khd", rounded, upstream, preferred_element_type=jnp.float32)
    spread = jnp.einsum("qhd,khd->hqk", upstream, values, preferred_element_type=jnp.float32)
    spread = lax.optimization_barrier(spread.astype(jnp.bfloat16)).astype(jnp.float32)
    score_grad = chances * (spread - jnp.sum(spread * chances, axis=-1, keepdims=True))
    score_grad = score_grad.astype(jnp.bfloat16)
    query_grad = (
        jnp.einsum("hqk,khd->qhd", score_grad, keys, preferred_element_type=jnp.float32)
        * score_scale
    )
    key_grad = (
        jnp.einsum("hqk,qhd->khd", score_grad, query, preferred_element_type=jnp.float32)
        * score_scale
    )
    return (
        query_grad.astype(jnp.bfloat16),
        key_grad.astype(jnp.bfloat16),
        value_grad.astype(jnp.bfloat16),
    )


def gelu_slope(before):
    return 0.5 * (1.0 + lax.erf(before * root_half)) + before * inv_root_two_pi * jnp.exp(
        -0.5 * before * before
    )


BLOCK = 384
CUBE = 16


def swap_cores(part):
    return part + lax.ppermute(part, "mp", [(0, 1), (1, 0)])


def hop(block, first, second, ranks):
    pairs = []
    for rank in range(ranks):
        pairs.append((2 * rank, 2 * (rank ^ first)))
        pairs.append((2 * rank + 1, 2 * (rank ^ second) + 1))
    return lax.ppermute(block, ("dp", "mp"), pairs)


def place():
    rank = lax.axis_index("dp")
    core = lax.axis_index("mp")
    x = rank & 1
    y = (rank >> 1) & 1
    z = ((rank >> 2) ^ (rank >> 3)) & 1
    swapped = core == 1
    return (jnp.where(swapped, y, x), z, jnp.where(swapped, x, y))


def cut_kernel(offsets, left_ref, right_ref, send_ref, keep_ref):
    for spot in range(8):
        left = left_ref[:, pl.ds(pl.multiple_of(offsets[spot], 128), BLOCK)]
        right = right_ref[:, pl.ds(pl.multiple_of(offsets[8 + spot], 128), BLOCK)]
        product = outer_sum(left, right)
        if spot < 4:
            keep_ref[spot] = product
        else:
            send_ref[spot - 4] = product


def cut_product(left, right, offsets):
    shape = jax.ShapeDtypeStruct((4, BLOCK, BLOCK), jnp.float32)
    return pl.pallas_call(
        cut_kernel,
        out_shape=(shape, shape),
        in_specs=[
            pl.BlockSpec(memory_space=pltpu.SMEM),
            pl.BlockSpec(memory_space=pltpu.VMEM),
            pl.BlockSpec(memory_space=pltpu.VMEM),
        ],
        out_specs=(pl.BlockSpec(memory_space=pltpu.VMEM), pl.BlockSpec(memory_space=pltpu.VMEM)),
        compiler_params=pltpu.CompilerParams(vmem_limit_bytes=24 << 20),
        cost_estimate=pl.CostEstimate(
            flops=16 * left.shape[0] * BLOCK * BLOCK,
            bytes_accessed=2 * (left.size + right.size) + 32 * BLOCK * BLOCK,
            transcendentals=0,
        ),
    )(offsets, left, right)


def join_kernel(layout, where_ref, near_ref, far_ref, *rest):
    outs, sem = rest[:-1], rest[-1]
    copies = []
    for block in range(8):
        out, row, column = layout[block]
        target = outs[out].at[pl.ds(row, BLOCK), pl.ds(column, BLOCK)]
        spot = where_ref[block]
        own = where_ref[8 + block]

        @pl.when(own == 0)
        def _(target=target, spot=spot, block=block):
            pltpu.make_async_copy(near_ref.at[spot], target, sem.at[block]).start()

        @pl.when(own != 0)
        def _(target=target, spot=spot, block=block):
            pltpu.make_async_copy(far_ref.at[spot], target, sem.at[block]).start()

        copies.append(pltpu.make_async_copy(near_ref.at[0], target, sem.at[block]))
    for copy in copies:
        copy.wait()


def join_blocks(near, far, layout, shapes, where):
    return pl.pallas_call(
        functools.partial(join_kernel, layout),
        out_shape=tuple(jax.ShapeDtypeStruct(shape, jnp.float32) for shape in shapes),
        in_specs=[
            pl.BlockSpec(memory_space=pltpu.SMEM),
            pl.BlockSpec(memory_space=pl.ANY),
            pl.BlockSpec(memory_space=pl.ANY),
        ],
        out_specs=tuple(pl.BlockSpec(memory_space=pl.ANY) for _ in shapes),
        scratch_shapes=[pltpu.SemaphoreType.DMA((8,))],
        cost_estimate=pl.CostEstimate(
            flops=0, bytes_accessed=64 * BLOCK * BLOCK, transcendentals=0
        ),
    )(where, near, far)


def dp_sum(send, keep, ranks):
    got = hop(send, 1, 2, ranks)
    part = keep[2:] + got[2:]
    low = hop(part, 4, 4, ranks)
    half = keep[1] + got[1] + low[1]
    quarter = hop(half, 2, 1, ranks)
    own = keep[0] + got[0] + low[0] + quarter
    total = own + hop(own, 12, 12, ranks)
    bit = CUBE
    while bit < ranks:
        total = total + hop(total, bit, bit, ranks)
        bit = 2 * bit
    other = hop(total, 2, 1, ranks)
    pair = jnp.stack([total, other])
    rest = hop(pair, 4, 4, ranks)
    near = jnp.concatenate([pair, rest])
    far = hop(near, 1, 2, ranks)
    return near, far


def dp_sum_small(value, ranks):
    for bit in (1, 2, 4, 12):
        value = value + hop(value, bit, bit, ranks)
    bit = CUBE
    while bit < ranks:
        value = value + hop(value, bit, bit, ranks)
        bit = 2 * bit
    return value


def body(
    ranks,
    tokens,
    lengths,
    cotangent,
    query_weight,
    query_bias,
    key_weight,
    value_weight,
    value_bias,
    out_weight,
    out_bias,
    mid_gain,
    mid_shift,
    up_weight,
    up_bias,
    down_weight,
    down_bias,
    final_gain,
    final_shift,
):
    first, second, third = place()
    mine = 4 * first + 2 * second + third
    spots = jnp.arange(8, dtype=jnp.int32)
    blocks = spots ^ mine
    rows_of = (blocks >> 1) * BLOCK
    columns_of = (blocks & 1) * BLOCK
    rest_left = jnp.where(blocks < 6, (blocks & 1) * BLOCK, 2 * BLOCK)
    rest_right = jnp.where(blocks < 6, (blocks >> 1) * BLOCK, (blocks - 3) * BLOCK)
    where = jnp.concatenate([blocks & 3, blocks >> 2]).astype(jnp.int32)
    rows = tokens.shape[0]
    pages = lengths.shape[0]
    length = rows // pages
    heads = query_weight.shape[1] // DH

    def by_page(matrix):
        return matrix.reshape(pages, length, heads, DH)

    query = (matmul(tokens, query_weight) + query_bias.astype(jnp.float32)).astype(jnp.bfloat16)
    keys = matmul(tokens, key_weight).astype(jnp.bfloat16)
    values = (matmul(tokens, value_weight) + value_bias.astype(jnp.float32)).astype(jnp.bfloat16)
    context, log_total = lax.map(
        attend_page, (by_page(query), by_page(keys), by_page(values), lengths)
    )
    context = context.reshape(rows, heads * DH)
    attended = swap_cores(matmul(context, out_weight))
    inputs = tokens.astype(jnp.float32)
    middle, mid_normal, mid_scale = norm_forward(
        inputs + attended + out_bias.astype(jnp.float32), mid_gain, mid_shift
    )
    mid_low = middle.astype(jnp.bfloat16)
    before = matmul(mid_low, up_weight) + up_bias.astype(jnp.float32)
    active = jax.nn.gelu(before, approximate=False).astype(jnp.bfloat16)
    down = swap_cores(matmul(active, down_weight))
    result, final_normal, final_scale = norm_forward(
        middle + down + down_bias.astype(jnp.float32), final_gain, final_shift
    )
    layer_out = result.astype(jnp.bfloat16)
    upper = cotangent.astype(jnp.float32)
    second_grad, final_gain_grad, final_shift_grad = norm_backward(
        upper, final_normal, final_scale, final_gain
    )
    down_bias_grad = jnp.sum(second_grad, axis=0)
    second_low = second_grad.astype(jnp.bfloat16)
    down_cut = cut_product(active, second_low, jnp.concatenate([rows_of, columns_of]))
    before_grad = (matmul_flip(second_low, down_weight) * gelu_slope(before)).astype(jnp.bfloat16)
    up_cut = cut_product(mid_low, before_grad, jnp.concatenate([columns_of, rows_of]))
    up_bias_grad = jnp.sum(before_grad.astype(jnp.float32), axis=0)
    mid_grad = second_grad + swap_cores(matmul_flip(before_grad, up_weight))
    first_grad, mid_gain_grad, mid_shift_grad = norm_backward(
        mid_grad, mid_normal, mid_scale, mid_gain
    )
    out_bias_grad = jnp.sum(first_grad, axis=0)
    first_low = first_grad.astype(jnp.bfloat16)
    context_grad = matmul_flip(first_low, out_weight).astype(jnp.bfloat16)
    query_grad, key_grad, value_grad = lax.map(
        attend_back,
        (by_page(query), by_page(keys), by_page(values), lengths, log_total, by_page(context_grad)),
    )
    query_grad = query_grad.reshape(rows, heads * DH)
    key_grad = key_grad.reshape(rows, heads * DH)
    value_grad = value_grad.reshape(rows, heads * DH)
    rest_cut = cut_product(
        jnp.concatenate([tokens, context], axis=1),
        jnp.concatenate([query_grad, key_grad, value_grad, first_low], axis=1),
        jnp.concatenate([rest_left, rest_right]),
    )
    query_bias_grad = jnp.sum(query_grad.astype(jnp.float32), axis=0)
    value_bias_grad = jnp.sum(value_grad.astype(jnp.float32), axis=0)
    input_part = (
        matmul_flip(query_grad, query_weight)
        + matmul_flip(key_grad, key_weight)
        + matmul_flip(value_grad, value_weight)
    )
    input_grad = (first_grad + swap_cores(input_part)).astype(jnp.bfloat16)
    small = jnp.concatenate(
        [
            query_bias_grad,
            value_bias_grad,
            up_bias_grad,
            out_bias_grad,
            mid_gain_grad,
            mid_shift_grad,
            down_bias_grad,
            final_gain_grad,
            final_shift_grad,
        ]
    ).reshape(-1, 384)
    small = dp_sum_small(small, ranks).reshape(-1)
    edges = [0, 384, 768, 2304, 3072, 3840, 4608, 5376, 6144, 6912]
    (
        query_bias_grad,
        value_bias_grad,
        up_bias_grad,
        out_bias_grad,
        mid_gain_grad,
        mid_shift_grad,
        down_bias_grad,
        final_gain_grad,
        final_shift_grad,
    ) = [small[low:high] for low, high in zip(edges[:-1], edges[1:])]
    width = tokens.shape[1]
    hidden = up_weight.shape[1]
    down_layout = [(0, (block >> 1) * BLOCK, (block & 1) * BLOCK) for block in range(8)]
    up_layout = [(0, (block & 1) * BLOCK, (block >> 1) * BLOCK) for block in range(8)]
    rest_layout = [(block >> 1, (block & 1) * BLOCK, 0) for block in range(6)] + [
        (3, 0, 0),
        (3, 0, BLOCK),
    ]
    (down_weight_grad,) = join_blocks(
        *dp_sum(*down_cut, ranks), down_layout, [(hidden, width)], where
    )
    (up_weight_grad,) = join_blocks(
        *dp_sum(*up_cut, ranks), up_layout, [(width, hidden)], where
    )
    query_weight_grad, key_weight_grad, value_weight_grad, out_weight_grad = join_blocks(
        *dp_sum(*rest_cut, ranks),
        rest_layout,
        [(width, heads * DH)] * 3 + [(heads * DH, width)],
        where,
    )
    return (
        layer_out,
        input_grad,
        query_weight_grad,
        query_bias_grad,
        key_weight_grad,
        value_weight_grad,
        value_bias_grad,
        out_weight_grad,
        out_bias_grad,
        mid_gain_grad,
        mid_shift_grad,
        up_weight_grad,
        up_bias_grad,
        down_weight_grad,
        down_bias_grad,
        final_gain_grad,
        final_shift_grad,
    )


def solution(mesh):
    in_specs = (
        P("dp", None),
        P("dp"),
        P("dp", None),
        P(None, "mp"),
        P("mp"),
        P(None, "mp"),
        P(None, "mp"),
        P("mp"),
        P("mp", None),
        P(),
        P(),
        P(),
        P(None, "mp"),
        P("mp"),
        P("mp", None),
        P(),
        P(),
        P(),
    )
    out_specs = (
        P("dp", None),
        P("dp", None),
        P(None, "mp"),
        P("mp"),
        P(None, "mp"),
        P(None, "mp"),
        P("mp"),
        P("mp", None),
        P(),
        P(),
        P(),
        P(None, "mp"),
        P("mp"),
        P("mp", None),
        P(),
        P(),
        P(),
    )
    return jax.shard_map(functools.partial(body, mesh.shape["dp"]), mesh=mesh, in_specs=in_specs, out_specs=out_specs, check_vma=False)
```

```python
import functools

import jax
import jax.numpy as jnp
import numpy as np
from jax import lax
from jax.experimental import pallas as pl
from jax.experimental.pallas import tpu as pltpu
from jax.sharding import PartitionSpec as P

DH = 64
BLOCK = 384
HALF = 192
CUBE = 16
MIB = 1 << 20

norm_eps = 1e-12
score_scale = 0.125
root_half = 0.7071067811865476
inv_root_two_pi = 0.3989422804014327

PLAN = {"D": "Q", "E": "P", "U": "P", "V": "P", "R": "S", "S": "P"}
ORDER = (
    ("D1", "E1", "keep", "ffn", "V1", "mid", "back", "cut", "tail", "E2", "D2", "V2", "U1", "S1", "E3", "V3"),
    ("R1", "E4", "D3", "V4", "E5", "R2", "E6", "D4", "S2", "V5", "R3", "U2", "R4", "D5", "V6", "S3"),
    ("U3", "E7", "R5", "V7", "S4", "R6", "D6", "U4", "S5", "Vj", "fin", "R7", "U5", "S6", "D7", "U6"),
    ("Ej", "S7", "Rj", "U7", "Sj", "Dj", "vec", "Uj"),
)
ROUTES = {
    "P": ((1, 2), (2, 1), (4, 4)),
    "S": ((1, 2), (4, 4), (2, 1)),
    "Q": ((4, 4), (1, 2), (2, 1)),
}
ACROSS = (12, 12)


def coordinate(rank, mask):
    if mask == 1:
        return rank & 1
    if mask == 2:
        return (rank >> 1) & 1
    return ((rank >> 2) ^ (rank >> 3)) & 1


def block_places(name):
    sub = HALF * (name in "EVS")
    places = []
    for block in range(8):
        high, low = block >> 1, block & 1
        if name in "DE":
            row, column = high * BLOCK + sub, low * BLOCK
            places.append((0, row, column, row, column))
        elif name in "UV":
            row, column = low * BLOCK + sub, high * BLOCK
            places.append((0, row, column, row, column))
        elif high < 3:
            row = low * BLOCK + sub
            places.append((high, row, 0, row, high * BLOCK))
        else:
            places.append((3, sub, low * BLOCK, 2 * BLOCK + sub, (3 + low) * BLOCK))
    return places


def device_tables(ranks):
    rows = []
    for rank in range(ranks):
        for core in range(2):
            row = []
            for name, route in PLAN.items():
                first, second, third = [coordinate(rank, pair[core]) for pair in ROUTES[route]]
                mine = 4 * first + 2 * second + third
                places = block_places(name)
                row += [places[spot ^ mine][3] for spot in range(8)]
                row += [places[spot ^ mine][4] for spot in range(8)]
                near = [(block ^ mine) & 3 for block in range(8)]
                far = list(near)
                for block in range(8):
                    edge = 4 if block < 4 else 3
                    if block >> 2 == first:
                        far[block] = near[edge]
                    else:
                        near[block] = (edge ^ mine) & 3
                row += near + far + [first]
            rows.append(row)
    return np.array(rows, np.int32)


TABLE = 33
PIECES = 4


def matmul(left, right):
    return jnp.dot(left, right, preferred_element_type=jnp.float32)


def matmul_flip(left, right):
    return lax.dot_general(
        left, right, (((1,), (1,)), ((), ())), preferred_element_type=jnp.float32
    )


def outer_sum(left, right):
    return lax.dot_general(
        left, right, (((0,), (0,)), ((), ())), preferred_element_type=jnp.float32
    )


def wide(ref):
    return ref[...].astype(jnp.float32)


def across(ref):
    return wide(ref).reshape(1, -1)


def row_mean(value):
    return jnp.mean(value, axis=-1, keepdims=True)


def norm_parts(value):
    center = value - row_mean(value)
    scale = lax.rsqrt(row_mean(center * center) + norm_eps)
    return center * scale, scale


def norm_lower(along, normal, scale):
    return scale * (along - row_mean(along) - normal * row_mean(along * normal))


def column_sum(value):
    return jnp.sum(value, axis=0, keepdims=True)


def cost(flops, bytes_accessed, transcendentals=0):
    return pl.CostEstimate(flops=1, bytes_accessed=1, transcendentals=0)


def call(kernel, ins, outs, estimate, limit, scalars=1, scratch=()):
    specs = [
        pl.BlockSpec(memory_space=pltpu.SMEM if place < scalars else pltpu.VMEM)
        for place in range(len(ins))
    ]
    return pl.pallas_call(
        kernel,
        out_shape=tuple(jax.ShapeDtypeStruct(shape, kind) for shape, kind in outs),
        in_specs=specs,
        out_specs=tuple(pl.BlockSpec(memory_space=pltpu.VMEM) for _ in outs),
        scratch_shapes=list(scratch),
        compiler_params=pltpu.CompilerParams(vmem_limit_bytes=limit * MIB),
        cost_estimate=estimate,
    )(*ins)


def head_of(lanes, head):
    return (lanes // DH) == head


def scores_flip(keys, query, limit):
    scores = matmul_flip(keys, query)
    visible = lax.broadcasted_iota(jnp.int32, scores.shape, 0) < limit
    return jnp.where(visible, scores, -1e30)


def attend_kernel(
    lengths, tokens, query_weight, query_bias, key_weight, value_weight, value_bias, out_weight,
    query_ref, keys_ref, values_ref, context_ref, log_ref, partial_ref,
):
    inputs = tokens[...]
    query_ref[...] = (matmul(inputs, query_weight[...]) + across(query_bias)).astype(jnp.bfloat16)
    keys_ref[...] = matmul(inputs, key_weight[...]).astype(jnp.bfloat16)
    values_ref[...] = (matmul(inputs, value_weight[...]) + across(value_bias)).astype(jnp.bfloat16)
    limit = lengths[0]
    for pair in range(query_ref.shape[1] // (2 * DH)):
        columns = slice(pair * 2 * DH, (pair + 1) * 2 * DH)
        query = query_ref[:, columns] * jnp.bfloat16(score_scale)
        keys = keys_ref[:, columns]
        values = values_ref[:, columns]
        lanes = lax.broadcasted_iota(jnp.int32, query.shape, 1)
        sides = []
        for head in range(2):
            scores = scores_flip(keys, jnp.where(head_of(lanes, head), query, 0), limit)
            top = jnp.max(scores, axis=0, keepdims=True)
            raised = jnp.exp(scores - top)
            total = jnp.sum(raised, axis=0, keepdims=True)
            chances = (raised * (1.0 / total)).astype(jnp.bfloat16)
            log_ref[2 * pair + head : 2 * pair + head + 1, :] = top + jnp.log(total)
            sides.append(outer_sum(values, chances))
        rows = lax.broadcasted_iota(jnp.int32, sides[0].shape, 0)
        context = jnp.where(head_of(rows, 0), sides[0], sides[1])
        context_ref[:, columns] = context.T.astype(jnp.bfloat16)
    partial_ref[...] = matmul(context_ref[...], out_weight[...])


def attend(lengths, tokens, query_weight, query_bias, key_weight, value_weight, value_bias, out_weight):
    rows, width = tokens.shape
    columns = query_weight.shape[1]
    narrow = ((rows, columns), jnp.bfloat16)
    return call(
        attend_kernel,
        (lengths, tokens, query_weight, query_bias, key_weight, value_weight, value_bias, out_weight),
        (narrow, narrow, narrow, narrow, ((8, rows), jnp.float32), ((rows, width), jnp.float32)),
        cost(8 * rows * width * columns + 8 * rows * rows * columns, 8 * MIB),
        limit=56,
    )


def phi(before):
    return 0.5 * (1.0 + lax.erf(before * root_half))


def ffn_kernel(
    tokens, own, got, out_bias, mid_gain, mid_shift, up_weight, up_bias, down_weight,
    normal_ref, scale_ref, low_ref, before_ref, active_ref, partial_ref,
):
    normal, scale = norm_parts(wide(tokens) + (own[...] + got[...]) + across(out_bias))
    normal_ref[...] = normal
    scale_ref[...] = scale
    low_ref[...] = (normal * across(mid_gain) + across(mid_shift)).astype(jnp.bfloat16)
    hidden = up_weight.shape[1]
    bias = across(up_bias)
    for start in range(0, hidden, 256):
        columns = slice(start, start + 256)
        before = matmul(low_ref[...], up_weight[:, columns]) + bias[:, columns]
        before_ref[:, columns] = before
        active_ref[:, columns] = (before * phi(before)).astype(jnp.bfloat16)
    partial_ref[...] = matmul(active_ref[...], down_weight[...])


def ffn(tokens, own, got, out_bias, mid_gain, mid_shift, up_weight, up_bias, down_weight):
    rows, width = tokens.shape
    hidden = up_weight.shape[1]
    full = ((rows, width), jnp.float32)
    return call(
        ffn_kernel,
        (tokens, own, got, out_bias, mid_gain, mid_shift, up_weight, up_bias, down_weight),
        (
            full,
            ((rows, 1), jnp.float32),
            ((rows, width), jnp.bfloat16),
            ((rows, hidden), jnp.float32),
            ((rows, hidden), jnp.bfloat16),
            full,
        ),
        cost(4 * rows * width * hidden, 16 * MIB, rows * hidden),
        scalars=0,
        limit=56,
    )


def cut(offsets, flipped, right, targets, first, spots):
    for part in range(2):
        base = (first + part) * TABLE
        for place, spot in enumerate(spots):
            row = pl.multiple_of(offsets[base + spot], HALF // 12)
            column = pl.multiple_of(offsets[base + 8 + spot], 128)
            targets[part][place * HALF : (place + 1) * HALF, :] = matmul(
                flipped[pl.ds(row, HALF), :], right[:, pl.ds(column, BLOCK)]
            )


KEPT = (0, 1, 2, 3)
SENT = (4, 5, 6, 7)


def flip_into(flipped, left, start=0):
    for column in range(0, left.shape[1], 128):
        flipped[start + column : start + column + 128, :] = left[:, column : column + 128].T


SUMS = 16
blocks = ((4 * HALF, BLOCK), jnp.float32)
blocks_and_sums = ((4 * HALF + 2 * SUMS, BLOCK), jnp.float32)


def sums(width):
    return ((8, width), jnp.float32)


def flip_kernel(value, flipped_ref):
    for column in range(0, value.shape[1], 128):
        flipped_ref[column : column + 128, :] = value[:, column : column + 128].T


def flip(value):
    return call(
        flip_kernel, (value,), ((value.shape[::-1], value.dtype),), cost(0, 4 * value.size), scalars=0, limit=56
    )[0]


def last_kernel(
    offsets, normal, mid_gain, mid_shift, own, got, down_bias, final_gain, cotangent, flipped,
    second_ref, low_ref, final_ref, send0, send1,
):
    middle = normal[...] * across(mid_gain) + across(mid_shift)
    final, scale = norm_parts(middle + (own[...] + got[...]) + across(down_bias))
    final_ref[...] = final
    second = norm_lower(wide(cotangent) * across(final_gain), final, scale)
    low_ref[...] = second.astype(jnp.bfloat16)
    second_ref[...] = second
    cut(offsets, flipped, low_ref, (send0, send1), 0, SENT)


def last(offsets, normal, mid_gain, mid_shift, own, got, down_bias, final_gain, cotangent, flipped):
    rows, width = normal.shape
    full = ((rows, width), jnp.float32)
    return call(
        last_kernel,
        (offsets, normal, mid_gain, mid_shift, own, got, down_bias, final_gain, cotangent, flipped),
        (full, ((rows, width), jnp.bfloat16), full, blocks, blocks),
        cost(rows * width * flipped.shape[0], 14 * MIB),
        limit=56,
    )


def keep_kernel(
    offsets, second, low, final, final_gain, final_shift, cotangent, flipped, out_ref, sums_ref, keep0, keep1
):
    cut(offsets, flipped, low, (keep0, keep1), 0, KEPT)
    upper = wide(cotangent)
    sums_ref[...] = jnp.zeros_like(sums_ref)
    sums_ref[0:1, :] = column_sum(second[...])
    sums_ref[1:2, :] = column_sum(upper * final[...])
    sums_ref[2:3, :] = column_sum(upper)
    out_ref[...] = (final[...] * across(final_gain) + across(final_shift)).astype(jnp.bfloat16)


def keep(offsets, second, low, final, final_gain, final_shift, cotangent, flipped):
    rows, width = low.shape
    return call(
        keep_kernel,
        (offsets, second, low, final, final_gain, final_shift, cotangent, flipped),
        (((rows, width), jnp.bfloat16), sums(width), blocks, blocks),
        cost(rows * width * flipped.shape[0], 14 * MIB),
        limit=26,
    )


def ffn_back_kernel(
    offsets, second_low, down_weight, before_ref, low, up_weight,
    sums_ref, send0, keep0, send1, keep1, *rest,
):
    partial_refs, before_grad, flipped = rest[:PIECES], rest[-2], rest[-1]
    hidden = before_ref.shape[1]
    width = sums_ref.shape[1]
    sums_ref[...] = jnp.zeros_like(sums_ref)
    for start in range(0, hidden, 256):
        columns = slice(start, start + 256)
        before = before_ref[:, columns]
        slope = phi(before) + before * inv_root_two_pi * jnp.exp(-0.5 * before * before)
        grad = (matmul_flip(second_low[...], down_weight[columns, :]) * slope).astype(jnp.bfloat16)
        before_grad[:, columns] = grad
        row, place = start // width, start % width
        sums_ref[row : row + 1, place : place + 256] = column_sum(grad.astype(jnp.float32))
    for place, partial_ref in enumerate(partial_refs):
        rows = slice(place * partial_ref.shape[0], (place + 1) * partial_ref.shape[0])
        partial_ref[...] = matmul_flip(before_grad[rows, :], up_weight[...])
    flip_into(flipped, low)
    cut(offsets, flipped, before_grad, (send0, send1), 2, SENT)
    cut(offsets, flipped, before_grad, (keep0, keep1), 2, KEPT)


def ffn_back(offsets, second_low, down_weight, before, low, up_weight):
    rows, width = low.shape
    hidden = before.shape[1]
    return call(
        ffn_back_kernel,
        (offsets, second_low, down_weight, before, low, up_weight),
        (sums(width), blocks, blocks, blocks, blocks) + (((rows // PIECES, width), jnp.float32),) * PIECES,
        cost(6 * rows * width * hidden, 18 * MIB, 2 * rows * hidden),
        scratch=[pltpu.VMEM((rows, hidden), jnp.bfloat16), pltpu.VMEM((width, rows), jnp.bfloat16)],
        limit=26,
    )


def mid_kernel(second, normal_ref, scale, mid_gain, out_weight, *rest):
    own, got = rest[:PIECES], rest[PIECES : 2 * PIECES]
    first_ref, low_ref, context_grad, sums_ref, upper = rest[2 * PIECES :]
    for place in range(PIECES):
        rows = slice(place * own[place].shape[0], (place + 1) * own[place].shape[0])
        upper[rows, :] = second[rows, :] + (own[place][...] + got[place][...])
    normal = normal_ref[...]
    sums_ref[...] = jnp.zeros_like(sums_ref)
    sums_ref[1:2, :] = column_sum(upper[...] * normal)
    sums_ref[2:3, :] = column_sum(upper[...])
    first = norm_lower(upper[...] * across(mid_gain), normal, scale[...])
    sums_ref[0:1, :] = column_sum(first)
    first_ref[...] = first
    low_ref[...] = first.astype(jnp.bfloat16)
    context_grad[...] = matmul_flip(low_ref[...], out_weight[...]).astype(jnp.bfloat16)


def mid(second, own, got, normal, scale, mid_gain, out_weight):
    rows, width = second.shape
    columns = out_weight.shape[0]
    return call(
        mid_kernel,
        (second, normal, scale, mid_gain, out_weight, *own, *got),
        (
            ((rows, width), jnp.float32),
            ((rows, width), jnp.bfloat16),
            ((rows, columns), jnp.bfloat16),
            sums(width),
        ),
        cost(2 * rows * width * columns, 10 * MIB),
        scalars=0,
        scratch=[pltpu.VMEM((rows, width), jnp.float32)],
        limit=20,
    )


def attend_back_kernel(
    lengths, query_ref, keys_ref, values_ref, log_ref, upstream_ref,
    grads_ref, sums_ref,
):
    limit = lengths[0]
    sums_ref[...] = jnp.zeros_like(sums_ref)
    width = query_ref.shape[1]
    for pair in range(width // (2 * DH)):
        columns = slice(pair * 2 * DH, (pair + 1) * 2 * DH)
        query = query_ref[:, columns] * jnp.bfloat16(score_scale)
        keys = keys_ref[:, columns]
        values = values_ref[:, columns]
        upstream = upstream_ref[:, columns]
        lanes = lax.broadcasted_iota(jnp.int32, query.shape, 1)
        value_grad = jnp.zeros(query.shape, jnp.float32)
        key_grad = jnp.zeros(query.shape, jnp.float32)
        sides = []
        for head in range(2):
            mine = head_of(lanes, head)
            asked = jnp.where(mine, query, 0)
            pulled = jnp.where(mine, upstream, 0)
            scores = scores_flip(keys, asked, limit)
            chances = jnp.exp(scores - log_ref[2 * pair + head : 2 * pair + head + 1, :])
            value_grad = value_grad + matmul(chances.astype(jnp.bfloat16), pulled)
            spread = matmul_flip(values, pulled).astype(jnp.bfloat16).astype(jnp.float32)
            common = jnp.sum(spread * chances, axis=0, keepdims=True)
            score_grad = (chances * (spread - common)).astype(jnp.bfloat16)
            key_grad = key_grad + matmul(score_grad, asked)
            sides.append(outer_sum(keys, score_grad))
        rows = lax.broadcasted_iota(jnp.int32, sides[0].shape, 0)
        query_grad = (jnp.where(head_of(rows, 0), sides[0], sides[1]).T * score_scale).astype(jnp.bfloat16)
        key_low = key_grad.astype(jnp.bfloat16)
        value_low = value_grad.astype(jnp.bfloat16)
        grads_ref[:, columns] = query_grad
        grads_ref[:, slice(width + columns.start, width + columns.stop)] = key_low
        grads_ref[:, slice(2 * width + columns.start, 2 * width + columns.stop)] = value_low
        sums_ref[0:1, columns] = column_sum(query_grad.astype(jnp.float32))
        sums_ref[0:1, slice(width + columns.start, width + columns.stop)] = column_sum(
            value_low.astype(jnp.float32)
        )


def attend_back(lengths, query, keys, values, log_total, upstream):
    rows, width = query.shape
    return call(
        attend_back_kernel,
        (lengths, query, keys, values, log_total, upstream),
        (((rows, 3 * width), jnp.bfloat16), sums(2 * width)),
        cost(20 * rows * rows * width, 4 * MIB, rows * rows * width // DH),
        limit=16,
    )


def rest_kernel(
    offsets, tokens, context, grads, first_low, last_sums, up_sums, mid_sums, back_sums,
    send0, keep0, send1, keep1, flipped, right,
):
    flip_into(flipped, tokens)
    flip_into(flipped, context, tokens.shape[1])
    right[:, : grads.shape[1]] = grads[...]
    right[:, grads.shape[1] :] = first_low[...]
    cut(offsets, flipped, right, (send0, send1), 4, SENT)
    cut(offsets, flipped, right, (keep0, keep1), 4, KEPT)
    rows = [last_sums[0:3, :], up_sums[0:2, :], mid_sums[0:3, :], back_sums[0:1, :]]
    send1[4 * HALF :, :] = jnp.zeros((2 * SUMS, BLOCK), jnp.float32)
    for half in range(2):
        place = 4 * HALF + half * SUMS
        for part in rows:
            send1[place : place + part.shape[0], :] = part[:, half * BLOCK : (half + 1) * BLOCK]
            place = place + part.shape[0]


def rest(offsets, tokens, context, grads, first_low, last_sums, up_sums, mid_sums, back_sums):
    rows, width = tokens.shape
    left = width + context.shape[1]
    right = grads.shape[1] + width
    return call(
        rest_kernel,
        (offsets, tokens, context, grads, first_low, last_sums, up_sums, mid_sums, back_sums),
        (blocks, blocks, blocks_and_sums, blocks),
        cost(32 * rows * HALF * BLOCK, 8 * MIB),
        scratch=[pltpu.VMEM((left, rows), jnp.bfloat16), pltpu.VMEM((rows, right), jnp.bfloat16)],
        limit=16,
    )


def input_kernel(grads, query_weight, key_weight, value_weight, partial_ref):
    width = query_weight.shape[1]
    partial_ref[...] = (
        matmul_flip(grads[:, :width], query_weight[...])
        + matmul_flip(grads[:, width : 2 * width], key_weight[...])
        + matmul_flip(grads[:, 2 * width :], value_weight[...])
    )


def input_part(grads, query_weight, key_weight, value_weight):
    rows, width = grads.shape[0], query_weight.shape[0]
    return call(
        input_kernel,
        (grads, query_weight, key_weight, value_weight),
        (((rows, width), jnp.float32),),
        cost(2 * rows * width * grads.shape[1], 6 * MIB),
        scalars=0,
        limit=10,
    )[0]


def join_kernel(name, table, near, far, *rest):
    places = block_places(name)
    count = len({place[0] for place in places})
    outs, done = rest[-count - 1 : -1], rest[-1]
    for side in range(2):

        @pl.when(table[16] == side)
        def _():
            copies = []
            for block in range(8):
                out, row, column = places[block][:3]
                source = near if block >> 2 == side else far
                copies.append(
                    pltpu.make_async_copy(
                        source.at[pl.ds(pl.multiple_of(table[8 * (source is far) + block] * HALF, 8), HALF)],
                        outs[out].at[pl.ds(row, HALF), pl.ds(column, BLOCK)],
                        done.at[block],
                    )
                )
            for copy in copies:
                copy.start()
            for copy in copies:
                copy.wait()


def join(name, table, near, far, shapes, earlier):
    specs = [
        pl.BlockSpec(memory_space=pltpu.SMEM),
        pl.BlockSpec(memory_space=pltpu.VMEM),
        pl.BlockSpec(memory_space=pltpu.VMEM),
    ] + [pl.BlockSpec(memory_space=pl.ANY) for _ in earlier]
    return pl.pallas_call(
        functools.partial(join_kernel, name),
        out_shape=tuple(jax.ShapeDtypeStruct(shape, jnp.float32) for shape in shapes),
        in_specs=specs,
        out_specs=tuple(pl.BlockSpec(memory_space=pl.ANY) for _ in shapes),
        scratch_shapes=[pltpu.SemaphoreType.DMA((8,))],
        input_output_aliases={3 + place: place for place in range(len(earlier))},
        compiler_params=pltpu.CompilerParams(vmem_limit_bytes=16 * MIB),
        cost_estimate=cost(0, 64 * HALF * BLOCK),
    )(table, near, far, *earlier)


def swap_cores(part):
    return lax.ppermute(part, "mp", [(0, 1), (1, 0)])


def hop(block, masks, ranks):
    pairs = [
        (2 * rank + core, 2 * (rank ^ masks[core]) + core) for rank in range(ranks) for core in (0, 1)
    ]
    return lax.ppermute(block, ("dp", "mp"), pairs)


def tied(value, before):
    return value if before is None else lax.optimization_barrier((value, before))[0]


class Sum:
    def __init__(self, name, send, keep, ranks):
        self.name, self.send, self.keep, self.ranks = name, send, keep, ranks
        self.masks = ROUTES[PLAN[name]] + (ACROSS,)
        self.got = {}
        self.extra = send[4 * HALF :] if send.shape[0] > 4 * HALF else None

    def with_extra(self, value, got, rows):
        if self.extra is None:
            return value
        self.extra = self.extra + got[rows:]
        return jnp.concatenate([value, self.extra])

    def step(self, number, before):
        got, one, two = self.got, HALF, 2 * HALF
        keep = tied(self.own if number > 4 else self.keep if number > 1 else self.send, before)
        if number == 1:
            value = keep
        elif number == 2:
            value = self.with_extra(keep[two:] + got[1][two : 2 * two], got[1], 2 * two)
        elif number == 3:
            value = self.with_extra(keep[one:two] + got[1][one:two] + got[2][one:two], got[2], two)
        elif number == 4:
            value = keep[:one] + got[1][:one] + got[2][:one] + got[3][:one]
            value = self.with_extra(value, got[3], one)
        elif number == 5:
            value = keep + got[4]
            bit = CUBE
            while bit < self.ranks:
                value = value + hop(value, (bit, bit), self.ranks)
                bit = 2 * bit
            if self.extra is not None:
                value, self.extra = value[:one], value[one:]
        elif number == 6:
            value = jnp.concatenate([keep, got[5]])
        else:
            value = jnp.concatenate([keep, got[6]])
        self.own = value
        with jax.named_scope(f"{self.name}{number}"):
            got[number] = hop(value, self.masks[min(number, 8 - number) - 1], self.ranks)
        return value


def body(
    ranks,
    tables,
    tokens,
    lengths,
    cotangent,
    query_weight,
    query_bias,
    key_weight,
    value_weight,
    value_bias,
    out_weight,
    out_bias,
    mid_gain,
    mid_shift,
    up_weight,
    up_bias,
    down_weight,
    down_bias,
    final_gain,
    final_shift,
):
    table = jnp.asarray(tables)[2 * lax.axis_index("dp") + lax.axis_index("mp")]
    width = tokens.shape[1]
    columns = query_weight.shape[1]
    hidden = up_weight.shape[1]

    query, keys, values, context, log_total, partial = attend(
        lengths, tokens, query_weight, query_bias, key_weight, value_weight, value_bias, out_weight
    )
    mid_normal, mid_scale, mid_low, before, active, down_partial = ffn(
        tokens, partial, swap_cores(partial), out_bias, mid_gain, mid_shift,
        up_weight, up_bias, down_weight,
    )
    active_flip = flip(active)
    second_grad, second_low, final_normal, *down_sent = last(
        table, mid_normal, mid_gain, mid_shift, down_partial, swap_cores(down_partial),
        down_bias, final_gain, cotangent, active_flip,
    )
    parts = {
        "D": Sum("D", down_sent[0], None, ranks),
        "E": Sum("E", down_sent[1], None, ranks),
    }
    point = None
    joined = {}
    for item in sum(ORDER, ()):
        if item == "keep":
            layer_out, last_sums, *down_kept = keep(
                table, second_grad, tied(second_low, point), final_normal, final_gain, final_shift,
                cotangent, active_flip,
            )
            parts["D"].keep, parts["E"].keep = down_kept
            point = down_kept[0]
        elif item == "ffn":
            up_sums, *up_cut = ffn_back(
                table, tied(second_low, point), down_weight, before, mid_low, up_weight
            )
            parts["U"] = Sum("U", up_cut[0], up_cut[1], ranks)
            parts["V"] = Sum("V", up_cut[2], up_cut[3], ranks)
            up_partial = up_cut[4:]
            up_got = [swap_cores(piece) for piece in up_partial]
            point = up_cut[0]
        elif item == "mid":
            first_grad, first_low, context_grad, mid_sums = mid(
                tied(second_grad, point), up_partial, up_got, mid_normal, mid_scale, mid_gain, out_weight
            )
            point = context_grad
        elif item == "back":
            grads, back_sums = attend_back(
                lengths, query, keys, values, log_total, tied(context_grad, point)
            )
            point = grads
        elif item == "cut":
            rest_cut = rest(
                table, tokens, context, tied(grads, point), first_low, last_sums, up_sums, mid_sums, back_sums
            )
            parts["R"] = Sum("R", rest_cut[0], rest_cut[1], ranks)
            parts["S"] = Sum("S", rest_cut[2], rest_cut[3], ranks)
            point = rest_cut[0]
        elif item == "tail":
            partial = input_part(tied(grads, point), query_weight, key_weight, value_weight)
            partial_got = swap_cores(partial)
            point = partial
        elif item == "fin":
            input_grad = (first_grad + (tied(partial, point) + partial_got)).astype(jnp.bfloat16)
            point = input_grad
        elif item == "vec":
            small = tied(parts["S"].extra, point).reshape(2, SUMS, BLOCK)
            small = jnp.concatenate([small[0], small[1]], axis=1)
            down_bias_grad, final_gain_grad, final_shift_grad = small[0], small[1], small[2]
            up_bias_grad = small[3 : 3 + hidden // width].reshape(-1)
            out_bias_grad, mid_gain_grad, mid_shift_grad = small[5], small[6], small[7]
            query_bias_grad, value_bias_grad = small[8, :columns], small[8, columns : 2 * columns]
            point = value_bias_grad
        elif item[1] == "j":
            family = {"E": "D", "V": "U", "S": "R"}.get(item[0], item[0])
            shapes = {
                "D": [(hidden, width)],
                "U": [(width, hidden)],
                "R": [(width, columns)] * 3 + [(columns, width)],
            }[family]
            place = list(PLAN).index(item[0]) * TABLE + 16
            part = parts[item[0]]
            joined[family] = join(
                item[0], table[place : place + 17], tied(part.own, point), part.got[7], shapes,
                joined.get(family, ()),
            )
            point = joined[family][0]
        else:
            point = parts[item[0]].step(int(item[1]), point)
    (down_weight_grad,), (up_weight_grad,) = joined["D"], joined["U"]
    query_weight_grad, key_weight_grad, value_weight_grad, out_weight_grad = joined["R"]
    return (
        layer_out,
        input_grad,
        query_weight_grad,
        query_bias_grad,
        key_weight_grad,
        value_weight_grad,
        value_bias_grad,
        out_weight_grad,
        out_bias_grad,
        mid_gain_grad,
        mid_shift_grad,
        up_weight_grad,
        up_bias_grad,
        down_weight_grad,
        down_bias_grad,
        final_gain_grad,
        final_shift_grad,
    )


def solution(mesh):
    rows, whole, split, vector = P("dp", None), P(), P(None, "mp"), P("mp")
    across = P("mp", None)
    in_specs = (
        rows, P("dp"), rows, split, vector, split, split, vector, across, whole, whole, whole,
        split, vector, across, whole, whole, whole,
    )
    out_specs = (
        rows, rows, split, vector, split, split, vector, across, whole, whole, whole,
        split, vector, across, whole, whole, whole,
    )
    ranks = mesh.shape["dp"]
    return jax.shard_map(
        functools.partial(body, ranks, device_tables(ranks)),
        mesh=mesh, in_specs=in_specs, out_specs=out_specs, check_vma=False,
    )
```

```python
import functools

import jax
import jax.numpy as jnp
import numpy as np
from jax import lax
from jax.experimental import pallas as pl
from jax.experimental.pallas import tpu as pltpu
from jax.sharding import PartitionSpec as P

DH = 64
BLOCK = 384
HALF = 192
CUBE = 16
MIB = 1 << 20

norm_eps = 1e-12
score_scale = 0.125
root_half = 0.7071067811865476
inv_root_two_pi = 0.3989422804014327

PLAN = {"D": "Q", "E": "P", "U": "P", "V": "P", "R": "S", "S": "P"}
ORDER = (
    ("D1", "E1", "keep", "ffn", "V1", "mid", "back", "tail", "E2", "D2", "V2", "cut", "S1", "U1", "E3", "V3"),
    ("R1", "E4", "D3", "V4", "E5", "R2", "E6", "D4", "V5", "S2", "R3", "U2", "R4", "D5", "V6", "S3"),
    ("U3", "E7", "R5", "V7", "S4", "R6", "D6", "U4", "S5", "Vj", "fin", "R7", "U5", "S6", "D7", "Ej"),
    ("U6", "S7", "Rj", "U7", "Sj", "Dj", "vec", "Uj"),
)
ROUTES = {
    "P": ((1, 2), (2, 1), (4, 4)),
    "S": ((1, 2), (4, 4), (2, 1)),
    "Q": ((4, 4), (1, 2), (2, 1)),
}
ACROSS = (12, 12)


def coordinate(rank, mask):
    if mask == 1:
        return rank & 1
    if mask == 2:
        return (rank >> 1) & 1
    return ((rank >> 2) ^ (rank >> 3)) & 1


def block_places(name):
    sub = HALF * (name in "EVS")
    places = []
    for block in range(8):
        high, low = block >> 1, block & 1
        if name in "DE":
            row, column = high * BLOCK + sub, low * BLOCK
            places.append((0, row, column, row, column))
        elif name in "UV":
            row, column = low * BLOCK + sub, high * BLOCK
            places.append((0, row, column, row, column))
        elif high < 3:
            row = low * BLOCK + sub
            places.append((high, row, 0, row, high * BLOCK))
        else:
            places.append((3, sub, low * BLOCK, 2 * BLOCK + sub, (3 + low) * BLOCK))
    return places


def device_tables(ranks):
    rows = []
    for rank in range(ranks):
        for core in range(2):
            row = []
            for name, route in PLAN.items():
                first, second, third = [coordinate(rank, pair[core]) for pair in ROUTES[route]]
                mine = 4 * first + 2 * second + third
                places = block_places(name)
                row += [places[spot ^ mine][3] for spot in range(8)]
                row += [places[spot ^ mine][4] for spot in range(8)]
                near = [(block ^ mine) & 3 for block in range(8)]
                far = list(near)
                for block in range(8):
                    edge = 4 if block < 4 else 3
                    if block >> 2 == first:
                        far[block] = near[edge]
                    else:
                        near[block] = (edge ^ mine) & 3
                row += near + far + [first]
            rows.append(row)
    return np.array(rows, np.int32)


TABLE = 33
PIECES = 4


def matmul(left, right):
    return jnp.dot(left, right, preferred_element_type=jnp.float32)


def matmul_flip(left, right):
    return lax.dot_general(
        left, right, (((1,), (1,)), ((), ())), preferred_element_type=jnp.float32
    )


def outer_sum(left, right):
    return lax.dot_general(
        left, right, (((0,), (0,)), ((), ())), preferred_element_type=jnp.float32
    )


def wide(ref):
    return ref[...].astype(jnp.float32)


def across(ref):
    return wide(ref).reshape(1, -1)


def row_mean(value):
    return jnp.mean(value, axis=-1, keepdims=True)


def norm_parts(value):
    center = value - row_mean(value)
    scale = lax.rsqrt(row_mean(center * center) + norm_eps)
    return center * scale, scale


def norm_lower(along, normal, scale):
    return scale * (along - row_mean(along) - normal * row_mean(along * normal))


def column_sum(value):
    return jnp.sum(value, axis=0, keepdims=True)


def cost(flops, bytes_accessed, transcendentals=0):
    return pl.CostEstimate(flops=1, bytes_accessed=1, transcendentals=0)


def call(kernel, ins, outs, estimate, limit, scalars=1, scratch=()):
    specs = [
        pl.BlockSpec(memory_space=pltpu.SMEM if place < scalars else pltpu.VMEM)
        for place in range(len(ins))
    ]
    return pl.pallas_call(
        kernel,
        out_shape=tuple(jax.ShapeDtypeStruct(shape, kind) for shape, kind in outs),
        in_specs=specs,
        out_specs=tuple(pl.BlockSpec(memory_space=pltpu.VMEM) for _ in outs),
        scratch_shapes=list(scratch),
        compiler_params=pltpu.CompilerParams(vmem_limit_bytes=limit * MIB),
        cost_estimate=estimate,
    )(*ins)


class Arrival:
    def __init__(self, source, target, sem):
        self.target = target
        self.copy = pltpu.make_async_copy(source, target, sem)
        self.copy.start()
        self.here = False
        self.shape = target.shape

    def wait(self):
        if not self.here:
            self.copy.wait()
            self.here = True

    def __getitem__(self, place):
        self.wait()
        return self.target[place]


class Departure:
    def __init__(self, source, target, sem):
        self.source = source
        self.copy = pltpu.make_async_copy(source, target, sem)
        self.shape = source.shape

    def __getitem__(self, place):
        return self.source[place]

    def __setitem__(self, place, value):
        self.source[place] = value

    def send(self):
        self.copy.start()


def mixed(kernel, ins, far_ins, outs, far_outs, estimate, limit, scalars=0, scratch=()):
    far_in = [pltpu.with_memory_space_constraint(array, pltpu.HBM) for array in far_ins]
    near_count, far_count, near_outs = len(ins), len(far_ins), len(outs)

    def body(*refs):
        near, refs = refs[:near_count], refs[near_count:]
        sources, refs = refs[:far_count], refs[far_count:]
        results, refs = refs[:near_outs], refs[near_outs:]
        targets, refs = refs[: len(far_outs)], refs[len(far_outs) :]
        held, refs = refs[:far_count], refs[far_count:]
        kept, refs = refs[: len(far_outs)], refs[len(far_outs) :]
        in_sem, out_sem = refs[:2]
        arrivals = [Arrival(sources[k], held[k], in_sem.at[k]) for k in range(far_count)]
        departures = [Departure(kept[k], targets[k], out_sem.at[k]) for k in range(len(far_outs))]
        kernel(*near, *arrivals, *results, *departures, *refs[2:])
        for departure in departures:
            departure.copy.wait()

    far, close = pl.BlockSpec(memory_space=pltpu.HBM), pl.BlockSpec(memory_space=pltpu.VMEM)
    small = pl.BlockSpec(memory_space=pltpu.SMEM)
    return pl.pallas_call(
        body,
        out_shape=tuple(jax.ShapeDtypeStruct(shape, kind) for shape, kind in outs)
        + tuple(pltpu.HBM(shape, kind) for shape, kind in far_outs),
        in_specs=[small] * scalars + [close] * (near_count - scalars) + [far] * far_count,
        out_specs=tuple([close] * near_outs + [far] * len(far_outs)),
        scratch_shapes=[pltpu.VMEM(array.shape, array.dtype) for array in far_ins]
        + [pltpu.VMEM(shape, kind) for shape, kind in far_outs]
        + [pltpu.SemaphoreType.DMA((max(1, far_count),)), pltpu.SemaphoreType.DMA((max(1, len(far_outs)),))]
        + list(scratch),
        compiler_params=pltpu.CompilerParams(vmem_limit_bytes=limit * MIB),
        cost_estimate=estimate,
    )(*ins, *far_in)


def head_of(lanes, head):
    return (lanes // DH) == head


def scores_flip(keys, query, limit):
    scores = matmul_flip(keys, query)
    visible = lax.broadcasted_iota(jnp.int32, scores.shape, 0) < limit
    return jnp.where(visible, scores, -1e30)


def attend_kernel(
    lengths, inputs, query_weight, query_bias, key_weight, value_weight, value_bias, out_weight, out_bias,
    partial_ref, query_ref, keys_ref, values_ref, context_ref, log_ref,
):
    query_ref[...] = (matmul(inputs[...], query_weight[...]) + across(query_bias)).astype(jnp.bfloat16)
    query_ref.send()
    keys_ref[...] = matmul(inputs[...], key_weight[...]).astype(jnp.bfloat16)
    keys_ref.send()
    values_ref[...] = (matmul(inputs[...], value_weight[...]) + across(value_bias)).astype(jnp.bfloat16)
    values_ref.send()
    limit = lengths[0]
    for pair in range(query_ref.shape[1] // (2 * DH)):
        columns = slice(pair * 2 * DH, (pair + 1) * 2 * DH)
        query = query_ref[:, columns] * jnp.bfloat16(score_scale)
        keys = keys_ref[:, columns]
        values = values_ref[:, columns]
        lanes = lax.broadcasted_iota(jnp.int32, query.shape, 1)
        sides = []
        for head in range(2):
            scores = scores_flip(keys, jnp.where(head_of(lanes, head), query, 0), limit)
            top = jnp.max(scores, axis=0, keepdims=True)
            raised = jnp.exp(scores - top)
            total = jnp.sum(raised, axis=0, keepdims=True)
            chances = (raised * (1.0 / total)).astype(jnp.bfloat16)
            log_ref[2 * pair + head : 2 * pair + head + 1, :] = top + jnp.log(total)
            sides.append(outer_sum(values, chances))
        rows = lax.broadcasted_iota(jnp.int32, sides[0].shape, 0)
        context = jnp.where(head_of(rows, 0), sides[0], sides[1])
        context_ref[:, columns] = context.T.astype(jnp.bfloat16)
    context_ref.send()
    log_ref.send()
    partial_ref[...] = matmul(context_ref[...], out_weight[...]) + 0.5 * across(out_bias)


def attend(
    lengths, tokens, query_weight, query_bias, key_weight, value_weight, value_bias, out_weight, out_bias
):
    rows, width = tokens.shape
    columns = query_weight.shape[1]
    partial, query, keys, values, context, log_total = mixed(
        attend_kernel,
        (lengths,),
        (tokens, query_weight, query_bias, key_weight, value_weight, value_bias, out_weight, out_bias),
        (((rows, width), jnp.float32),),
        [((rows, columns), jnp.bfloat16)] * 4 + [((8, rows), jnp.float32)],
        cost(8 * rows * width * columns + 8 * rows * rows * columns, 8 * MIB),
        limit=20,
        scalars=1,
    )
    return query, keys, values, context, log_total, partial


def phi(before):
    return 0.5 * (1.0 + lax.erf(before * root_half))


def ffn_kernel(
    tokens, own, got, up_weight, mid_gain, mid_shift, up_bias, down_weight, down_bias,
    partial_ref, middle_ref, normal_ref, scale_ref, low_ref, flipped_ref, active,
):
    normal, scale = norm_parts(wide(tokens) + (own[...] + got[...]))
    middle = normal * across(mid_gain) + across(mid_shift)
    middle_ref[...] = middle
    middle_ref.send()
    low_ref[...] = middle.astype(jnp.bfloat16)
    low_ref.send()
    normal_ref[...] = normal
    normal_ref.send()
    scale_ref[...] = scale
    scale_ref.send()
    hidden = up_weight.shape[1]
    bias = across(up_bias)
    for start in range(0, hidden, 256):
        columns = slice(start, start + 256)
        before = matmul(low_ref[...], up_weight[:, columns]) + bias[:, columns]
        active[:, columns] = (before * phi(before)).astype(jnp.bfloat16)
    flip_into(flipped_ref, active)
    flipped_ref.send()
    partial_ref[...] = matmul(active[...], down_weight[...]) + 0.5 * across(down_bias)


def ffn(tokens, own, got, mid_gain, mid_shift, up_weight, up_bias, down_weight, down_bias):
    rows, width = tokens.shape
    hidden = up_weight.shape[1]
    full = ((rows, width), jnp.float32)
    return mixed(
        ffn_kernel,
        (tokens, own, got, up_weight),
        (mid_gain, mid_shift, up_bias, down_weight, down_bias),
        (full,),
        (full, full, ((rows, 1), jnp.float32), ((rows, width), jnp.bfloat16), ((hidden, rows), jnp.bfloat16)),
        cost(4 * rows * width * hidden, 16 * MIB, rows * hidden),
        limit=26,
        scratch=[pltpu.VMEM((rows, hidden), jnp.bfloat16)],
    )


def cut(offsets, flipped, right, targets, first, spots):
    for part in range(2):
        base = (first + part) * TABLE
        for place, spot in enumerate(spots):
            row = pl.multiple_of(offsets[base + spot], HALF // 12)
            column = pl.multiple_of(offsets[base + 8 + spot], 128)
            targets[part][place * HALF : (place + 1) * HALF, :] = matmul(
                flipped[pl.ds(row, HALF), :], right[:, pl.ds(column, BLOCK)]
            )


KEPT = (0, 1, 2, 3)
SENT = (4, 5, 6, 7)


def flip_into(flipped, left, start=0):
    for column in range(0, left.shape[1], 128):
        flipped[start + column : start + column + 128, :] = left[:, column : column + 128].T


SUMS = 16
blocks = ((4 * HALF, BLOCK), jnp.float32)
blocks_and_sums = ((4 * HALF + 2 * SUMS, BLOCK), jnp.float32)


def sums(width):
    return ((8, width), jnp.float32)


def last_kernel(
    offsets, middle, own, got, cotangent, final_gain, flipped,
    second_ref, low_ref, final_ref, send0, send1,
):
    final, scale = norm_parts(middle[...] + (own[...] + got[...]))
    final_ref[...] = final
    second = norm_lower(wide(cotangent) * across(final_gain), final, scale)
    low_ref[...] = second.astype(jnp.bfloat16)
    second_ref[...] = second
    flipped.wait()
    cut(offsets, flipped.target, low_ref, (send0, send1), 0, SENT)


def last(offsets, middle, own, got, cotangent, final_gain, flipped):
    rows, width = middle.shape
    full = ((rows, width), jnp.float32)
    return mixed(
        last_kernel,
        (offsets, middle, own, got),
        (cotangent, final_gain, flipped),
        (full, ((rows, width), jnp.bfloat16), full, blocks, blocks),
        (),
        cost(rows * width * flipped.shape[0], 14 * MIB),
        limit=24,
        scalars=1,
    )


def keep_kernel(
    offsets, second, low, final, final_gain, final_shift, cotangent, flipped, out_ref, sums_ref, keep0, keep1
):
    cut(offsets, flipped, low, (keep0, keep1), 0, KEPT)
    upper = wide(cotangent)
    sums_ref[...] = jnp.zeros_like(sums_ref)
    sums_ref[0:1, :] = column_sum(second[...])
    sums_ref[1:2, :] = column_sum(upper * final[...])
    sums_ref[2:3, :] = column_sum(upper)
    out_ref[...] = (final[...] * across(final_gain) + across(final_shift)).astype(jnp.bfloat16)


def keep(offsets, second, low, final, final_gain, final_shift, cotangent, flipped):
    rows, width = low.shape
    return call(
        keep_kernel,
        (offsets, second, low, final, final_gain, final_shift, cotangent, flipped),
        (((rows, width), jnp.bfloat16), sums(width), blocks, blocks),
        cost(rows * width * flipped.shape[0], 14 * MIB),
        limit=26,
    )


def ffn_back_kernel(
    offsets, second_low, down_weight, low, up_weight, up_bias,
    sums_ref, send0, keep0, send1, keep1, *rest,
):
    partial_refs, before_grad, flipped = rest[:PIECES], rest[-2], rest[-1]
    hidden = up_weight.shape[1]
    width = sums_ref.shape[1]
    bias = across(up_bias)
    sums_ref[...] = jnp.zeros_like(sums_ref)
    for start in range(0, hidden, 256):
        columns = slice(start, start + 256)
        before = matmul(low[...], up_weight[:, columns]) + bias[:, columns]
        slope = phi(before) + before * inv_root_two_pi * jnp.exp(-0.5 * before * before)
        grad = (matmul_flip(second_low[...], down_weight[columns, :]) * slope).astype(jnp.bfloat16)
        before_grad[:, columns] = grad
        row, place = start // width, start % width
        sums_ref[row : row + 1, place : place + 256] = column_sum(grad.astype(jnp.float32))
    for place, partial_ref in enumerate(partial_refs):
        rows = slice(place * partial_ref.shape[0], (place + 1) * partial_ref.shape[0])
        partial_ref[...] = matmul_flip(before_grad[rows, :], up_weight[...])
    flip_into(flipped, low)
    cut(offsets, flipped, before_grad, (send0, send1), 2, SENT)
    cut(offsets, flipped, before_grad, (keep0, keep1), 2, KEPT)


def ffn_back(offsets, second_low, down_weight, low, up_weight, up_bias):
    rows, width = low.shape
    hidden = up_weight.shape[1]
    return call(
        ffn_back_kernel,
        (offsets, second_low, down_weight, low, up_weight, up_bias),
        (sums(width), blocks, blocks, blocks, blocks) + (((rows // PIECES, width), jnp.float32),) * PIECES,
        cost(6 * rows * width * hidden, 18 * MIB, 2 * rows * hidden),
        scratch=[pltpu.VMEM((rows, hidden), jnp.bfloat16), pltpu.VMEM((width, rows), jnp.bfloat16)],
        limit=26,
    )


def mid_kernel(second, normal_ref, scale, mid_gain, out_weight, *rest):
    own, got = rest[:PIECES], rest[PIECES : 2 * PIECES]
    first_ref, low_ref, context_grad, sums_ref, upper = rest[2 * PIECES :]
    for place in range(PIECES):
        rows = slice(place * own[place].shape[0], (place + 1) * own[place].shape[0])
        upper[rows, :] = second[rows, :] + (own[place][...] + got[place][...])
    normal = normal_ref[...]
    sums_ref[...] = jnp.zeros_like(sums_ref)
    sums_ref[1:2, :] = column_sum(upper[...] * normal)
    sums_ref[2:3, :] = column_sum(upper[...])
    first = norm_lower(upper[...] * across(mid_gain), normal, scale[...])
    sums_ref[0:1, :] = column_sum(first)
    first_ref[...] = first
    low_ref[...] = first.astype(jnp.bfloat16)
    context_grad[...] = matmul_flip(low_ref[...], out_weight[...]).astype(jnp.bfloat16)


def mid(second, own, got, normal, scale, mid_gain, out_weight):
    rows, width = second.shape
    columns = out_weight.shape[0]
    return call(
        mid_kernel,
        (second, normal, scale, mid_gain, out_weight, *own, *got),
        (
            ((rows, width), jnp.float32),
            ((rows, width), jnp.bfloat16),
            ((rows, columns), jnp.bfloat16),
            sums(width),
        ),
        cost(2 * rows * width * columns, 10 * MIB),
        scalars=0,
        scratch=[pltpu.VMEM((rows, width), jnp.float32)],
        limit=20,
    )


def attend_back_kernel(
    lengths, query_ref, keys_ref, values_ref, log_ref, upstream_ref,
    grads_ref, sums_ref,
):
    limit = lengths[0]
    sums_ref[...] = jnp.zeros_like(sums_ref)
    width = query_ref.shape[1]
    for pair in range(width // (2 * DH)):
        columns = slice(pair * 2 * DH, (pair + 1) * 2 * DH)
        query = query_ref[:, columns] * jnp.bfloat16(score_scale)
        keys = keys_ref[:, columns]
        values = values_ref[:, columns]
        upstream = upstream_ref[:, columns]
        lanes = lax.broadcasted_iota(jnp.int32, query.shape, 1)
        value_grad = jnp.zeros(query.shape, jnp.float32)
        key_grad = jnp.zeros(query.shape, jnp.float32)
        sides = []
        for head in range(2):
            mine = head_of(lanes, head)
            asked = jnp.where(mine, query, 0)
            pulled = jnp.where(mine, upstream, 0)
            scores = scores_flip(keys, asked, limit)
            chances = jnp.exp(scores - log_ref[2 * pair + head : 2 * pair + head + 1, :])
            value_grad = value_grad + matmul(chances.astype(jnp.bfloat16), pulled)
            spread = matmul_flip(values, pulled).astype(jnp.bfloat16).astype(jnp.float32)
            common = jnp.sum(spread * chances, axis=0, keepdims=True)
            score_grad = (chances * (spread - common)).astype(jnp.bfloat16)
            key_grad = key_grad + matmul(score_grad, asked)
            sides.append(outer_sum(keys, score_grad))
        rows = lax.broadcasted_iota(jnp.int32, sides[0].shape, 0)
        query_grad = (jnp.where(head_of(rows, 0), sides[0], sides[1]).T * score_scale).astype(jnp.bfloat16)
        key_low = key_grad.astype(jnp.bfloat16)
        value_low = value_grad.astype(jnp.bfloat16)
        grads_ref[:, columns] = query_grad
        grads_ref[:, slice(width + columns.start, width + columns.stop)] = key_low
        grads_ref[:, slice(2 * width + columns.start, 2 * width + columns.stop)] = value_low
        sums_ref[0:1, columns] = column_sum(query_grad.astype(jnp.float32))
        sums_ref[0:1, slice(width + columns.start, width + columns.stop)] = column_sum(
            value_low.astype(jnp.float32)
        )


def attend_back(lengths, query, keys, values, log_total, upstream):
    rows, width = query.shape
    return call(
        attend_back_kernel,
        (lengths, query, keys, values, log_total, upstream),
        (((rows, 3 * width), jnp.bfloat16), sums(2 * width)),
        cost(20 * rows * rows * width, 4 * MIB, rows * rows * width // DH),
        limit=16,
    )


def rest_kernel(
    offsets, tokens, context, grads, first_low, last_sums, up_sums, mid_sums, back_sums,
    send0, keep0, send1, keep1, flipped, right,
):
    flip_into(flipped, tokens)
    flip_into(flipped, context, tokens.shape[1])
    right[:, : grads.shape[1]] = grads[...]
    right[:, grads.shape[1] :] = first_low[...]
    cut(offsets, flipped, right, (send0, send1), 4, SENT)
    cut(offsets, flipped, right, (keep0, keep1), 4, KEPT)
    rows = [last_sums[0:3, :], up_sums[0:2, :], mid_sums[0:3, :], back_sums[0:1, :]]
    send1[4 * HALF :, :] = jnp.zeros((2 * SUMS, BLOCK), jnp.float32)
    for half in range(2):
        place = 4 * HALF + half * SUMS
        for part in rows:
            send1[place : place + part.shape[0], :] = part[:, half * BLOCK : (half + 1) * BLOCK]
            place = place + part.shape[0]


def rest(offsets, tokens, context, grads, first_low, last_sums, up_sums, mid_sums, back_sums):
    rows, width = tokens.shape
    left = width + context.shape[1]
    right = grads.shape[1] + width
    return call(
        rest_kernel,
        (offsets, tokens, context, grads, first_low, last_sums, up_sums, mid_sums, back_sums),
        (blocks, blocks, blocks_and_sums, blocks),
        cost(32 * rows * HALF * BLOCK, 8 * MIB),
        scratch=[pltpu.VMEM((left, rows), jnp.bfloat16), pltpu.VMEM((rows, right), jnp.bfloat16)],
        limit=16,
    )


def input_kernel(grads, query_weight, key_weight, value_weight, partial_ref):
    width = query_weight.shape[1]
    partial_ref[...] = (
        matmul_flip(grads[:, :width], query_weight[...])
        + matmul_flip(grads[:, width : 2 * width], key_weight[...])
        + matmul_flip(grads[:, 2 * width :], value_weight[...])
    )


def input_part(grads, query_weight, key_weight, value_weight):
    rows, width = grads.shape[0], query_weight.shape[0]
    return call(
        input_kernel,
        (grads, query_weight, key_weight, value_weight),
        (((rows, width), jnp.float32),),
        cost(2 * rows * width * grads.shape[1], 6 * MIB),
        scalars=0,
        limit=10,
    )[0]


def join_kernel(name, table, near, far, *rest):
    places = block_places(name)
    count = len({place[0] for place in places})
    outs, done = rest[-count - 1 : -1], rest[-1]
    for side in range(2):

        @pl.when(table[16] == side)
        def _():
            copies = []
            for block in range(8):
                out, row, column = places[block][:3]
                source = near if block >> 2 == side else far
                copies.append(
                    pltpu.make_async_copy(
                        source.at[pl.ds(pl.multiple_of(table[8 * (source is far) + block] * HALF, 8), HALF)],
                        outs[out].at[pl.ds(row, HALF), pl.ds(column, BLOCK)],
                        done.at[block],
                    )
                )
            for copy in copies:
                copy.start()
            for copy in copies:
                copy.wait()


def join(name, table, near, far, shapes, earlier):
    specs = [
        pl.BlockSpec(memory_space=pltpu.SMEM),
        pl.BlockSpec(memory_space=pltpu.VMEM),
        pl.BlockSpec(memory_space=pltpu.VMEM),
    ] + [pl.BlockSpec(memory_space=pl.ANY) for _ in earlier]
    return pl.pallas_call(
        functools.partial(join_kernel, name),
        out_shape=tuple(jax.ShapeDtypeStruct(shape, jnp.float32) for shape in shapes),
        in_specs=specs,
        out_specs=tuple(pl.BlockSpec(memory_space=pl.ANY) for _ in shapes),
        scratch_shapes=[pltpu.SemaphoreType.DMA((8,))],
        input_output_aliases={3 + place: place for place in range(len(earlier))},
        compiler_params=pltpu.CompilerParams(vmem_limit_bytes=16 * MIB),
        cost_estimate=cost(0, 64 * HALF * BLOCK),
    )(table, near, far, *earlier)


def swap_cores(part):
    return lax.ppermute(part, "mp", [(0, 1), (1, 0)])


def hop(block, masks, ranks):
    pairs = [
        (2 * rank + core, 2 * (rank ^ masks[core]) + core) for rank in range(ranks) for core in (0, 1)
    ]
    return lax.ppermute(block, ("dp", "mp"), pairs)


def tied(value, before):
    return value if before is None else lax.optimization_barrier((value, before))[0]


class Sum:
    def __init__(self, name, send, keep, ranks):
        self.name, self.send, self.keep, self.ranks = name, send, keep, ranks
        self.masks = ROUTES[PLAN[name]] + (ACROSS,)
        self.got = {}
        self.extra = send[4 * HALF :] if send.shape[0] > 4 * HALF else None

    def with_extra(self, value, got, rows):
        if self.extra is None:
            return value
        self.extra = self.extra + got[rows:]
        return jnp.concatenate([value, self.extra])

    def step(self, number, before):
        got, one, two = self.got, HALF, 2 * HALF
        keep = tied(self.own if number > 4 else self.keep if number > 1 else self.send, before)
        if number == 1:
            value = keep
        elif number == 2:
            value = self.with_extra(keep[two:] + got[1][two : 2 * two], got[1], 2 * two)
        elif number == 3:
            value = self.with_extra(keep[one:two] + got[1][one:two] + got[2][one:two], got[2], two)
        elif number == 4:
            value = keep[:one] + got[1][:one] + got[2][:one] + got[3][:one]
            value = self.with_extra(value, got[3], one)
        elif number == 5:
            value = keep + got[4]
            bit = CUBE
            while bit < self.ranks:
                value = value + hop(value, (bit, bit), self.ranks)
                bit = 2 * bit
            if self.extra is not None:
                value, self.extra = value[:one], value[one:]
        elif number == 6:
            value = jnp.concatenate([keep, got[5]])
        else:
            value = jnp.concatenate([keep, got[6]])
        self.own = value
        with jax.named_scope(f"{self.name}{number}"):
            got[number] = hop(value, self.masks[min(number, 8 - number) - 1], self.ranks)
        return value


def body(
    ranks,
    tables,
    tokens,
    lengths,
    cotangent,
    query_weight,
    query_bias,
    key_weight,
    value_weight,
    value_bias,
    out_weight,
    out_bias,
    mid_gain,
    mid_shift,
    up_weight,
    up_bias,
    down_weight,
    down_bias,
    final_gain,
    final_shift,
):
    table = jnp.asarray(tables)[2 * lax.axis_index("dp") + lax.axis_index("mp")]
    width = tokens.shape[1]
    columns = query_weight.shape[1]
    hidden = up_weight.shape[1]

    query, keys, values, context, log_total, partial = attend(
        lengths, tokens, query_weight, query_bias, key_weight, value_weight, value_bias, out_weight, out_bias
    )
    down_partial, middle, mid_normal, mid_scale, mid_low, active_flip = ffn(
        tokens, partial, swap_cores(partial), mid_gain, mid_shift, up_weight, up_bias, down_weight, down_bias
    )
    second_grad, second_low, final_normal, *down_sent = last(
        table, middle, down_partial, swap_cores(down_partial), cotangent, final_gain, active_flip
    )
    parts = {
        "D": Sum("D", down_sent[0], None, ranks),
        "E": Sum("E", down_sent[1], None, ranks),
    }
    point = None
    joined = {}
    for item in sum(ORDER, ()):
        if item == "keep":
            layer_out, last_sums, *down_kept = keep(
                table, second_grad, tied(second_low, point), final_normal, final_gain, final_shift,
                cotangent, active_flip,
            )
            parts["D"].keep, parts["E"].keep = down_kept
            point = down_kept[0]
        elif item == "ffn":
            up_sums, *up_cut = ffn_back(
                table, tied(second_low, point), down_weight, mid_low, up_weight, up_bias
            )
            parts["U"] = Sum("U", up_cut[0], up_cut[1], ranks)
            parts["V"] = Sum("V", up_cut[2], up_cut[3], ranks)
            up_partial = up_cut[4:]
            up_got = [swap_cores(piece) for piece in up_partial]
            point = up_cut[0]
        elif item == "mid":
            first_grad, first_low, context_grad, mid_sums = mid(
                tied(second_grad, point), up_partial, up_got, mid_normal, mid_scale, mid_gain, out_weight
            )
            point = context_grad
        elif item == "back":
            grads, back_sums = attend_back(
                lengths, query, keys, values, log_total, tied(context_grad, point)
            )
            point = grads
        elif item == "cut":
            rest_cut = rest(
                table, tokens, context, tied(grads, point), first_low, last_sums, up_sums, mid_sums, back_sums
            )
            parts["R"] = Sum("R", rest_cut[0], rest_cut[1], ranks)
            parts["S"] = Sum("S", rest_cut[2], rest_cut[3], ranks)
            point = rest_cut[0]
        elif item == "tail":
            partial = input_part(tied(grads, point), query_weight, key_weight, value_weight)
            partial_got = swap_cores(partial)
            point = partial
        elif item == "fin":
            input_grad = (first_grad + (tied(partial, point) + partial_got)).astype(jnp.bfloat16)
            point = input_grad
        elif item == "vec":
            small = tied(parts["S"].extra, point).reshape(2, SUMS, BLOCK)
            small = jnp.concatenate([small[0], small[1]], axis=1)
            down_bias_grad, final_gain_grad, final_shift_grad = small[0], small[1], small[2]
            up_bias_grad = small[3 : 3 + hidden // width].reshape(-1)
            out_bias_grad, mid_gain_grad, mid_shift_grad = small[5], small[6], small[7]
            query_bias_grad, value_bias_grad = small[8, :columns], small[8, columns : 2 * columns]
            point = value_bias_grad
        elif item[1] == "j":
            family = {"E": "D", "V": "U", "S": "R"}.get(item[0], item[0])
            shapes = {
                "D": [(hidden, width)],
                "U": [(width, hidden)],
                "R": [(width, columns)] * 3 + [(columns, width)],
            }[family]
            place = list(PLAN).index(item[0]) * TABLE + 16
            part = parts[item[0]]
            joined[family] = join(
                item[0], table[place : place + 17], tied(part.own, point), part.got[7], shapes,
                joined.get(family, ()),
            )
            point = joined[family][0]
        else:
            point = parts[item[0]].step(int(item[1]), point)
    (down_weight_grad,), (up_weight_grad,) = joined["D"], joined["U"]
    query_weight_grad, key_weight_grad, value_weight_grad, out_weight_grad = joined["R"]
    return (
        layer_out,
        input_grad,
        query_weight_grad,
        query_bias_grad,
        key_weight_grad,
        value_weight_grad,
        value_bias_grad,
        out_weight_grad,
        out_bias_grad,
        mid_gain_grad,
        mid_shift_grad,
        up_weight_grad,
        up_bias_grad,
        down_weight_grad,
        down_bias_grad,
        final_gain_grad,
        final_shift_grad,
    )


def solution(mesh):
    rows, whole, split, vector = P("dp", None), P(), P(None, "mp"), P("mp")
    across = P("mp", None)
    in_specs = (
        rows, P("dp"), rows, split, vector, split, split, vector, across, whole, whole, whole,
        split, vector, across, whole, whole, whole,
    )
    out_specs = (
        rows, rows, split, vector, split, split, vector, across, whole, whole, whole,
        split, vector, across, whole, whole, whole,
    )
    ranks = mesh.shape["dp"]
    return jax.shard_map(
        functools.partial(body, ranks, device_tables(ranks)),
        mesh=mesh, in_specs=in_specs, out_specs=out_specs, check_vma=False,
    )
```

```python
import functools

import jax
import jax.numpy as jnp
import numpy as np
from jax import lax
from jax.experimental import pallas as pl
from jax.experimental.pallas import tpu as pltpu
from jax.sharding import PartitionSpec as P

DH = 64
BLOCK = 384
HALF = 192
CUBE = 16
MIB = 1 << 20

norm_eps = 1e-12
score_scale = 0.125
root_half = 0.7071067811865476
inv_root_two_pi = 0.3989422804014327

PLAN = {"D": "Q", "E": "P", "U": "P", "V": "P", "R": "S", "S": "P"}
ORDER = (
    ("D1", "E1", "keep", "ffn", "V1", "mid", "back", "tail", "E2", "D2", "V2", "cut", "S1", "U1", "E3", "V3"),
    ("R1", "E4", "D3", "V4", "E5", "R2", "E6", "D4", "V5", "S2", "R3", "U2", "R4", "D5", "V6", "S3"),
    ("U3", "E7", "R5", "V7", "S4", "R6", "D6", "U4", "S5", "Vj", "fin", "R7", "U5", "S6", "D7", "Ej"),
    ("U6", "S7", "Rj", "U7", "Sj", "Dj", "vec", "Uj"),
)
ROUTES = {
    "P": ((1, 2), (2, 1), (4, 4)),
    "S": ((1, 2), (4, 4), (2, 1)),
    "Q": ((4, 4), (1, 2), (2, 1)),
}
ACROSS = (12, 12)


def coordinate(rank, mask):
    if mask == 1:
        return rank & 1
    if mask == 2:
        return (rank >> 1) & 1
    return ((rank >> 2) ^ (rank >> 3)) & 1


def block_places(name):
    sub = HALF * (name in "EVS")
    places = []
    for block in range(8):
        high, low = block >> 1, block & 1
        if name in "DE":
            row, column = high * BLOCK + sub, low * BLOCK
            places.append((0, row, column, row, column))
        elif name in "UV":
            row, column = low * BLOCK + sub, high * BLOCK
            places.append((0, row, column, row, column))
        elif high < 3:
            row = low * BLOCK + sub
            places.append((high, row, 0, row, high * BLOCK))
        else:
            places.append((3, sub, low * BLOCK, 2 * BLOCK + sub, (3 + low) * BLOCK))
    return places


def device_tables(ranks):
    rows = []
    for rank in range(ranks):
        for core in range(2):
            row = []
            for name, route in PLAN.items():
                first, second, third = [coordinate(rank, pair[core]) for pair in ROUTES[route]]
                mine = 4 * first + 2 * second + third
                places = block_places(name)
                row += [places[spot ^ mine][3] for spot in range(8)]
                row += [places[spot ^ mine][4] for spot in range(8)]
                near = [(block ^ mine) & 3 for block in range(8)]
                far = list(near)
                for block in range(8):
                    edge = 4 if block < 4 else 3
                    if block >> 2 == first:
                        far[block] = near[edge]
                    else:
                        near[block] = (edge ^ mine) & 3
                row += near + far + [first]
            rows.append(row)
    return np.array(rows, np.int32)


TABLE = 33
PIECES = 4


def matmul(left, right):
    return jnp.dot(left, right, preferred_element_type=jnp.float32)


def matmul_flip(left, right):
    return lax.dot_general(
        left, right, (((1,), (1,)), ((), ())), preferred_element_type=jnp.float32
    )


def outer_sum(left, right):
    return lax.dot_general(
        left, right, (((0,), (0,)), ((), ())), preferred_element_type=jnp.float32
    )


def wide(ref):
    return ref[...].astype(jnp.float32)


def across(ref):
    return wide(ref).reshape(1, -1)


def row_mean(value):
    return jnp.mean(value, axis=-1, keepdims=True)


def norm_parts(value):
    center = value - row_mean(value)
    scale = lax.rsqrt(row_mean(center * center) + norm_eps)
    return center * scale, scale


def norm_lower(along, normal, scale):
    return scale * (along - row_mean(along) - normal * row_mean(along * normal))


def column_sum(value):
    return jnp.sum(value, axis=0, keepdims=True)


def cost(flops, bytes_accessed, transcendentals=0):
    return pl.CostEstimate(flops=1, bytes_accessed=1, transcendentals=0)


def call(kernel, ins, outs, estimate, limit, scalars=1, scratch=()):
    specs = [
        pl.BlockSpec(memory_space=pltpu.SMEM if place < scalars else pltpu.VMEM)
        for place in range(len(ins))
    ]
    return pl.pallas_call(
        kernel,
        out_shape=tuple(jax.ShapeDtypeStruct(shape, kind) for shape, kind in outs),
        in_specs=specs,
        out_specs=tuple(pl.BlockSpec(memory_space=pltpu.VMEM) for _ in outs),
        scratch_shapes=list(scratch),
        compiler_params=pltpu.CompilerParams(vmem_limit_bytes=limit * MIB),
        cost_estimate=estimate,
    )(*ins)


class Arrival:
    def __init__(self, source, target, sem):
        self.target = target
        self.copy = pltpu.make_async_copy(source, target, sem)
        self.copy.start()
        self.here = False
        self.shape = target.shape

    def wait(self):
        if not self.here:
            self.copy.wait()
            self.here = True

    def __getitem__(self, place):
        self.wait()
        return self.target[place]


class Departure:
    def __init__(self, source, target, sem):
        self.source = source
        self.copy = pltpu.make_async_copy(source, target, sem)
        self.shape = source.shape

    def __getitem__(self, place):
        return self.source[place]

    def __setitem__(self, place, value):
        self.source[place] = value

    def send(self):
        self.copy.start()


def mixed(kernel, ins, far_ins, outs, far_outs, estimate, limit, scalars=0, scratch=()):
    far_in = [pltpu.with_memory_space_constraint(array, pltpu.HBM) for array in far_ins]
    near_count, far_count, near_outs = len(ins), len(far_ins), len(outs)

    def body(*refs):
        near, refs = refs[:near_count], refs[near_count:]
        sources, refs = refs[:far_count], refs[far_count:]
        results, refs = refs[:near_outs], refs[near_outs:]
        targets, refs = refs[: len(far_outs)], refs[len(far_outs) :]
        held, refs = refs[:far_count], refs[far_count:]
        kept, refs = refs[: len(far_outs)], refs[len(far_outs) :]
        in_sem, out_sem = refs[:2]
        arrivals = [Arrival(sources[k], held[k], in_sem.at[k]) for k in range(far_count)]
        departures = [Departure(kept[k], targets[k], out_sem.at[k]) for k in range(len(far_outs))]
        kernel(*near, *arrivals, *results, *departures, *refs[2:])
        for departure in departures:
            departure.copy.wait()

    far, close = pl.BlockSpec(memory_space=pltpu.HBM), pl.BlockSpec(memory_space=pltpu.VMEM)
    small = pl.BlockSpec(memory_space=pltpu.SMEM)
    return pl.pallas_call(
        body,
        out_shape=tuple(jax.ShapeDtypeStruct(shape, kind) for shape, kind in outs)
        + tuple(pltpu.HBM(shape, kind) for shape, kind in far_outs),
        in_specs=[small] * scalars + [close] * (near_count - scalars) + [far] * far_count,
        out_specs=tuple([close] * near_outs + [far] * len(far_outs)),
        scratch_shapes=[pltpu.VMEM(array.shape, array.dtype) for array in far_ins]
        + [pltpu.VMEM(shape, kind) for shape, kind in far_outs]
        + [pltpu.SemaphoreType.DMA((max(1, far_count),)), pltpu.SemaphoreType.DMA((max(1, len(far_outs)),))]
        + list(scratch),
        compiler_params=pltpu.CompilerParams(vmem_limit_bytes=limit * MIB),
        cost_estimate=estimate,
    )(*ins, *far_in)


def head_of(lanes, head):
    return (lanes // DH) == head


def scores_flip(keys, query, limit):
    scores = matmul_flip(keys, query)
    visible = lax.broadcasted_iota(jnp.int32, scores.shape, 0) < limit
    return jnp.where(visible, scores, -1e30)


def attend_kernel(
    lengths, inputs, query_weight, query_bias, key_weight, value_weight, value_bias, out_weight, out_bias,
    partial_ref, query_ref, keys_ref, values_ref, context_ref, log_ref,
):
    query_ref[...] = (matmul(inputs[...], query_weight[...]) + across(query_bias)).astype(jnp.bfloat16)
    query_ref.send()
    keys_ref[...] = matmul(inputs[...], key_weight[...]).astype(jnp.bfloat16)
    keys_ref.send()
    values_ref[...] = (matmul(inputs[...], value_weight[...]) + across(value_bias)).astype(jnp.bfloat16)
    values_ref.send()
    limit = lengths[0]
    for pair in range(query_ref.shape[1] // (2 * DH)):
        columns = slice(pair * 2 * DH, (pair + 1) * 2 * DH)
        query = query_ref[:, columns] * jnp.bfloat16(score_scale)
        keys = keys_ref[:, columns]
        values = values_ref[:, columns]
        lanes = lax.broadcasted_iota(jnp.int32, query.shape, 1)
        sides = []
        for head in range(2):
            scores = scores_flip(keys, jnp.where(head_of(lanes, head), query, 0), limit)
            top = jnp.max(scores, axis=0, keepdims=True)
            raised = jnp.exp(scores - top)
            total = jnp.sum(raised, axis=0, keepdims=True)
            chances = (raised * (1.0 / total)).astype(jnp.bfloat16)
            log_ref[2 * pair + head : 2 * pair + head + 1, :] = top + jnp.log(total)
            sides.append(outer_sum(values, chances))
        rows = lax.broadcasted_iota(jnp.int32, sides[0].shape, 0)
        context = jnp.where(head_of(rows, 0), sides[0], sides[1])
        context_ref[:, columns] = context.T.astype(jnp.bfloat16)
    context_ref.send()
    log_ref.send()
    partial_ref[...] = matmul(context_ref[...], out_weight[...]) + 0.5 * across(out_bias)


def attend(
    lengths, tokens, query_weight, query_bias, key_weight, value_weight, value_bias, out_weight, out_bias
):
    rows, width = tokens.shape
    columns = query_weight.shape[1]
    partial, query, keys, values, context, log_total = mixed(
        attend_kernel,
        (lengths,),
        (tokens, query_weight, query_bias, key_weight, value_weight, value_bias, out_weight, out_bias),
        (((rows, width), jnp.float32),),
        [((rows, columns), jnp.bfloat16)] * 4 + [((8, rows), jnp.float32)],
        cost(8 * rows * width * columns + 8 * rows * rows * columns, 8 * MIB),
        limit=20,
        scalars=1,
    )
    return query, keys, values, context, log_total, partial


def phi(before):
    return 0.5 * (1.0 + lax.erf(before * root_half))


def ffn_kernel(
    tokens, own, got, up_weight, mid_gain, mid_shift, up_bias, down_weight, down_bias,
    partial_ref, middle_ref, normal_ref, scale_ref, low_ref, flipped_ref, active,
):
    normal, scale = norm_parts(wide(tokens) + (own[...] + got[...]))
    middle = normal * across(mid_gain) + across(mid_shift)
    middle_ref[...] = middle
    middle_ref.send()
    low_ref[...] = middle.astype(jnp.bfloat16)
    low_ref.send()
    normal_ref[...] = normal
    normal_ref.send()
    scale_ref[...] = scale
    scale_ref.send()
    hidden = up_weight.shape[1]
    bias = across(up_bias)
    for start in range(0, hidden, 256):
        columns = slice(start, start + 256)
        before = matmul(low_ref[...], up_weight[:, columns]) + bias[:, columns]
        active[:, columns] = (before * phi(before)).astype(jnp.bfloat16)
    flip_into(flipped_ref, active)
    flipped_ref.send()
    partial_ref[...] = matmul(active[...], down_weight[...]) + 0.5 * across(down_bias)


def ffn(tokens, own, got, mid_gain, mid_shift, up_weight, up_bias, down_weight, down_bias):
    rows, width = tokens.shape
    hidden = up_weight.shape[1]
    full = ((rows, width), jnp.float32)
    return mixed(
        ffn_kernel,
        (tokens, own, got, up_weight),
        (mid_gain, mid_shift, up_bias, down_weight, down_bias),
        (full,),
        (full, full, ((rows, 1), jnp.float32), ((rows, width), jnp.bfloat16), ((hidden, rows), jnp.bfloat16)),
        cost(4 * rows * width * hidden, 16 * MIB, rows * hidden),
        limit=26,
        scratch=[pltpu.VMEM((rows, hidden), jnp.bfloat16)],
    )


def cut(offsets, flipped, right, targets, first, spots):
    for part in range(2):
        base = (first + part) * TABLE
        for place, spot in enumerate(spots):
            row = pl.multiple_of(offsets[base + spot], HALF // 12)
            column = pl.multiple_of(offsets[base + 8 + spot], 128)
            targets[part][place * HALF : (place + 1) * HALF, :] = matmul(
                flipped[pl.ds(row, HALF), :], right[:, pl.ds(column, BLOCK)]
            )


KEPT = (0, 1, 2, 3)
SENT = (4, 5, 6, 7)


def flip_into(flipped, left, start=0):
    for column in range(0, left.shape[1], 128):
        flipped[start + column : start + column + 128, :] = left[:, column : column + 128].T


SUMS = 16
blocks = ((4 * HALF, BLOCK), jnp.float32)
blocks_and_sums = ((4 * HALF + 2 * SUMS, BLOCK), jnp.float32)


def sums(width):
    return ((8, width), jnp.float32)


def last_kernel(
    offsets, middle, own, got, cotangent, final_gain, flipped,
    second_ref, low_ref, final_ref, send0, send1,
):
    final, scale = norm_parts(middle[...] + (own[...] + got[...]))
    final_ref[...] = final
    second = norm_lower(wide(cotangent) * across(final_gain), final, scale)
    low_ref[...] = second.astype(jnp.bfloat16)
    second_ref[...] = second
    flipped.wait()
    cut(offsets, flipped.target, low_ref, (send0, send1), 0, SENT)


def last(offsets, middle, own, got, cotangent, final_gain, flipped):
    rows, width = middle.shape
    full = ((rows, width), jnp.float32)
    return mixed(
        last_kernel,
        (offsets, middle, own, got),
        (cotangent, final_gain, flipped),
        (full, ((rows, width), jnp.bfloat16), full, blocks, blocks),
        (),
        cost(rows * width * flipped.shape[0], 14 * MIB),
        limit=24,
        scalars=1,
    )


def keep_kernel(
    offsets, second, low, final, final_gain, final_shift, cotangent, flipped, out_ref, sums_ref, keep0, keep1
):
    cut(offsets, flipped, low, (keep0, keep1), 0, KEPT)
    upper = wide(cotangent)
    sums_ref[...] = jnp.zeros_like(sums_ref)
    sums_ref[0:1, :] = column_sum(second[...])
    sums_ref[1:2, :] = column_sum(upper * final[...])
    sums_ref[2:3, :] = column_sum(upper)
    out_ref[...] = (final[...] * across(final_gain) + across(final_shift)).astype(jnp.bfloat16)


def keep(offsets, second, low, final, final_gain, final_shift, cotangent, flipped):
    rows, width = low.shape
    return call(
        keep_kernel,
        (offsets, second, low, final, final_gain, final_shift, cotangent, flipped),
        (((rows, width), jnp.bfloat16), sums(width), blocks, blocks),
        cost(rows * width * flipped.shape[0], 14 * MIB),
        limit=26,
    )


def ffn_back_kernel(
    offsets, second_low, down_weight, low, up_weight, up_bias,
    sums_ref, send0, keep0, send1, keep1, *rest,
):
    partial_refs, before_grad, flipped = rest[:PIECES], rest[-2], rest[-1]
    hidden = up_weight.shape[1]
    width = sums_ref.shape[1]
    bias = across(up_bias)
    sums_ref[...] = jnp.zeros_like(sums_ref)
    for start in range(0, hidden, 256):
        columns = slice(start, start + 256)
        before = matmul(low[...], up_weight[:, columns]) + bias[:, columns]
        slope = phi(before) + before * inv_root_two_pi * jnp.exp(-0.5 * before * before)
        grad = (matmul_flip(second_low[...], down_weight[columns, :]) * slope).astype(jnp.bfloat16)
        before_grad[:, columns] = grad
        row, place = start // width, start % width
        sums_ref[row : row + 1, place : place + 256] = column_sum(grad.astype(jnp.float32))
    for place, partial_ref in enumerate(partial_refs):
        rows = slice(place * partial_ref.shape[0], (place + 1) * partial_ref.shape[0])
        partial_ref[...] = matmul_flip(before_grad[rows, :], up_weight[...])
    flip_into(flipped, low)
    cut(offsets, flipped, before_grad, (send0, send1), 2, SENT)
    cut(offsets, flipped, before_grad, (keep0, keep1), 2, KEPT)


def ffn_back(offsets, second_low, down_weight, low, up_weight, up_bias):
    rows, width = low.shape
    hidden = up_weight.shape[1]
    return call(
        ffn_back_kernel,
        (offsets, second_low, down_weight, low, up_weight, up_bias),
        (sums(width), blocks, blocks, blocks, blocks) + (((rows // PIECES, width), jnp.float32),) * PIECES,
        cost(6 * rows * width * hidden, 18 * MIB, 2 * rows * hidden),
        scratch=[pltpu.VMEM((rows, hidden), jnp.bfloat16), pltpu.VMEM((width, rows), jnp.bfloat16)],
        limit=26,
    )


def mid_kernel(second, normal_ref, scale, mid_gain, out_weight, *rest):
    own, got = rest[:PIECES], rest[PIECES : 2 * PIECES]
    first_ref, low_ref, context_grad, sums_ref, upper = rest[2 * PIECES :]
    for place in range(PIECES):
        rows = slice(place * own[place].shape[0], (place + 1) * own[place].shape[0])
        upper[rows, :] = second[rows, :] + (own[place][...] + got[place][...])
    normal = normal_ref[...]
    sums_ref[...] = jnp.zeros_like(sums_ref)
    sums_ref[1:2, :] = column_sum(upper[...] * normal)
    sums_ref[2:3, :] = column_sum(upper[...])
    first = norm_lower(upper[...] * across(mid_gain), normal, scale[...])
    sums_ref[0:1, :] = column_sum(first)
    first_ref[...] = first
    low_ref[...] = first.astype(jnp.bfloat16)
    context_grad[...] = matmul_flip(low_ref[...], out_weight[...]).astype(jnp.bfloat16)


def mid(second, own, got, normal, scale, mid_gain, out_weight):
    rows, width = second.shape
    columns = out_weight.shape[0]
    return call(
        mid_kernel,
        (second, normal, scale, mid_gain, out_weight, *own, *got),
        (
            ((rows, width), jnp.float32),
            ((rows, width), jnp.bfloat16),
            ((rows, columns), jnp.bfloat16),
            sums(width),
        ),
        cost(2 * rows * width * columns, 10 * MIB),
        scalars=0,
        scratch=[pltpu.VMEM((rows, width), jnp.float32)],
        limit=20,
    )


def attend_back_kernel(
    lengths, query_ref, keys_ref, values_ref, log_ref, upstream_ref,
    grads_ref, sums_ref,
):
    limit = lengths[0]
    sums_ref[...] = jnp.zeros_like(sums_ref)
    width = query_ref.shape[1]
    @pl.loop(0, width // (2 * DH))
    def _(pair):
        start = pl.multiple_of(pair * 2 * DH, 2 * DH)
        columns = pl.ds(start, 2 * DH)
        query = query_ref[:, columns] * jnp.bfloat16(score_scale)
        keys = keys_ref[:, columns]
        values = values_ref[:, columns]
        upstream = upstream_ref[:, columns]
        lanes = lax.broadcasted_iota(jnp.int32, query.shape, 1)
        value_grad = jnp.zeros(query.shape, jnp.float32)
        key_grad = jnp.zeros(query.shape, jnp.float32)
        sides = []
        for head in range(2):
            mine = head_of(lanes, head)
            asked = jnp.where(mine, query, 0)
            pulled = jnp.where(mine, upstream, 0)
            scores = scores_flip(keys, asked, limit)
            chances = jnp.exp(scores - log_ref[pl.ds(2 * pair + head, 1), :])
            value_grad = value_grad + matmul(chances.astype(jnp.bfloat16), pulled)
            spread = matmul_flip(values, pulled).astype(jnp.bfloat16).astype(jnp.float32)
            common = jnp.sum(spread * chances, axis=0, keepdims=True)
            score_grad = (chances * (spread - common)).astype(jnp.bfloat16)
            key_grad = key_grad + matmul(score_grad, asked)
            sides.append(outer_sum(keys, score_grad))
        rows = lax.broadcasted_iota(jnp.int32, sides[0].shape, 0)
        query_grad = (jnp.where(head_of(rows, 0), sides[0], sides[1]).T * score_scale).astype(jnp.bfloat16)
        key_low = key_grad.astype(jnp.bfloat16)
        value_low = value_grad.astype(jnp.bfloat16)
        grads_ref[:, columns] = query_grad
        grads_ref[:, pl.ds(width + start, 2 * DH)] = key_low
        grads_ref[:, pl.ds(2 * width + start, 2 * DH)] = value_low
        sums_ref[0:1, columns] = column_sum(query_grad.astype(jnp.float32))
        sums_ref[0:1, pl.ds(width + start, 2 * DH)] = column_sum(
            value_low.astype(jnp.float32)
        )


def attend_back(lengths, query, keys, values, log_total, upstream):
    rows, width = query.shape
    return call(
        attend_back_kernel,
        (lengths, query, keys, values, log_total, upstream),
        (((rows, 3 * width), jnp.bfloat16), sums(2 * width)),
        cost(20 * rows * rows * width, 4 * MIB, rows * rows * width // DH),
        limit=16,
    )


def rest_kernel(
    offsets, tokens, context, grads, first_low, last_sums, up_sums, mid_sums, back_sums,
    send0, keep0, send1, keep1, flipped, right,
):
    flip_into(flipped, tokens)
    flip_into(flipped, context, tokens.shape[1])
    right[:, : grads.shape[1]] = grads[...]
    right[:, grads.shape[1] :] = first_low[...]
    cut(offsets, flipped, right, (send0, send1), 4, SENT)
    cut(offsets, flipped, right, (keep0, keep1), 4, KEPT)
    rows = [last_sums[0:3, :], up_sums[0:2, :], mid_sums[0:3, :], back_sums[0:1, :]]
    send1[4 * HALF :, :] = jnp.zeros((2 * SUMS, BLOCK), jnp.float32)
    for half in range(2):
        place = 4 * HALF + half * SUMS
        for part in rows:
            send1[place : place + part.shape[0], :] = part[:, half * BLOCK : (half + 1) * BLOCK]
            place = place + part.shape[0]


def rest(offsets, tokens, context, grads, first_low, last_sums, up_sums, mid_sums, back_sums):
    rows, width = tokens.shape
    left = width + context.shape[1]
    right = grads.shape[1] + width
    return call(
        rest_kernel,
        (offsets, tokens, context, grads, first_low, last_sums, up_sums, mid_sums, back_sums),
        (blocks, blocks, blocks_and_sums, blocks),
        cost(32 * rows * HALF * BLOCK, 8 * MIB),
        scratch=[pltpu.VMEM((left, rows), jnp.bfloat16), pltpu.VMEM((rows, right), jnp.bfloat16)],
        limit=16,
    )


def input_kernel(grads, query_weight, key_weight, value_weight, partial_ref):
    width = query_weight.shape[1]
    partial_ref[...] = (
        matmul_flip(grads[:, :width], query_weight[...])
        + matmul_flip(grads[:, width : 2 * width], key_weight[...])
        + matmul_flip(grads[:, 2 * width :], value_weight[...])
    )


def input_part(grads, query_weight, key_weight, value_weight):
    rows, width = grads.shape[0], query_weight.shape[0]
    return call(
        input_kernel,
        (grads, query_weight, key_weight, value_weight),
        (((rows, width), jnp.float32),),
        cost(2 * rows * width * grads.shape[1], 6 * MIB),
        scalars=0,
        limit=10,
    )[0]


def join_kernel(name, table, near, far, *rest):
    places = block_places(name)
    count = len({place[0] for place in places})
    outs, done = rest[-count - 1 : -1], rest[-1]
    for side in range(2):

        @pl.when(table[16] == side)
        def _():
            copies = []
            for block in range(8):
                out, row, column = places[block][:3]
                source = near if block >> 2 == side else far
                copies.append(
                    pltpu.make_async_copy(
                        source.at[pl.ds(pl.multiple_of(table[8 * (source is far) + block] * HALF, 8), HALF)],
                        outs[out].at[pl.ds(row, HALF), pl.ds(column, BLOCK)],
                        done.at[block],
                    )
                )
            for copy in copies:
                copy.start()
            for copy in copies:
                copy.wait()


def join(name, table, near, far, shapes, earlier):
    specs = [
        pl.BlockSpec(memory_space=pltpu.SMEM),
        pl.BlockSpec(memory_space=pltpu.VMEM),
        pl.BlockSpec(memory_space=pltpu.VMEM),
    ] + [pl.BlockSpec(memory_space=pl.ANY) for _ in earlier]
    return pl.pallas_call(
        functools.partial(join_kernel, name),
        out_shape=tuple(jax.ShapeDtypeStruct(shape, jnp.float32) for shape in shapes),
        in_specs=specs,
        out_specs=tuple(pl.BlockSpec(memory_space=pl.ANY) for _ in shapes),
        scratch_shapes=[pltpu.SemaphoreType.DMA((8,))],
        input_output_aliases={3 + place: place for place in range(len(earlier))},
        compiler_params=pltpu.CompilerParams(vmem_limit_bytes=16 * MIB),
        cost_estimate=cost(0, 64 * HALF * BLOCK),
    )(table, near, far, *earlier)


def swap_cores(part):
    return lax.ppermute(part, "mp", [(0, 1), (1, 0)])


def hop(block, masks, ranks):
    pairs = [
        (2 * rank + core, 2 * (rank ^ masks[core]) + core) for rank in range(ranks) for core in (0, 1)
    ]
    return lax.ppermute(block, ("dp", "mp"), pairs)


def tied(value, before):
    return value if before is None else lax.optimization_barrier((value, before))[0]


class Sum:
    def __init__(self, name, send, keep, ranks):
        self.name, self.send, self.keep, self.ranks = name, send, keep, ranks
        self.masks = ROUTES[PLAN[name]] + (ACROSS,)
        self.got = {}
        self.extra = send[4 * HALF :] if send.shape[0] > 4 * HALF else None

    def with_extra(self, value, got, rows):
        if self.extra is None:
            return value
        self.extra = self.extra + got[rows:]
        return jnp.concatenate([value, self.extra])

    def step(self, number, before):
        got, one, two = self.got, HALF, 2 * HALF
        keep = tied(self.own if number > 4 else self.keep if number > 1 else self.send, before)
        if number == 1:
            value = keep
        elif number == 2:
            value = self.with_extra(keep[two:] + got[1][two : 2 * two], got[1], 2 * two)
        elif number == 3:
            value = self.with_extra(keep[one:two] + got[1][one:two] + got[2][one:two], got[2], two)
        elif number == 4:
            value = keep[:one] + got[1][:one] + got[2][:one] + got[3][:one]
            value = self.with_extra(value, got[3], one)
        elif number == 5:
            value = keep + got[4]
            bit = CUBE
            while bit < self.ranks:
                value = value + hop(value, (bit, bit), self.ranks)
                bit = 2 * bit
            if self.extra is not None:
                value, self.extra = value[:one], value[one:]
        elif number == 6:
            value = jnp.concatenate([keep, got[5]])
        else:
            value = jnp.concatenate([keep, got[6]])
        self.own = value
        with jax.named_scope(f"{self.name}{number}"):
            got[number] = hop(value, self.masks[min(number, 8 - number) - 1], self.ranks)
        return value


def body(
    ranks,
    tables,
    tokens,
    lengths,
    cotangent,
    query_weight,
    query_bias,
    key_weight,
    value_weight,
    value_bias,
    out_weight,
    out_bias,
    mid_gain,
    mid_shift,
    up_weight,
    up_bias,
    down_weight,
    down_bias,
    final_gain,
    final_shift,
):
    table = jnp.asarray(tables)[2 * lax.axis_index("dp") + lax.axis_index("mp")]
    width = tokens.shape[1]
    columns = query_weight.shape[1]
    hidden = up_weight.shape[1]

    query, keys, values, context, log_total, partial = attend(
        lengths, tokens, query_weight, query_bias, key_weight, value_weight, value_bias, out_weight, out_bias
    )
    down_partial, middle, mid_normal, mid_scale, mid_low, active_flip = ffn(
        tokens, partial, swap_cores(partial), mid_gain, mid_shift, up_weight, up_bias, down_weight, down_bias
    )
    second_grad, second_low, final_normal, *down_sent = last(
        table, middle, down_partial, swap_cores(down_partial), cotangent, final_gain, active_flip
    )
    parts = {
        "D": Sum("D", down_sent[0], None, ranks),
        "E": Sum("E", down_sent[1], None, ranks),
    }
    point = None
    joined = {}
    for item in sum(ORDER, ()):
        if item == "keep":
            layer_out, last_sums, *down_kept = keep(
                table, second_grad, tied(second_low, point), final_normal, final_gain, final_shift,
                cotangent, active_flip,
            )
            parts["D"].keep, parts["E"].keep = down_kept
            point = down_kept[0]
        elif item == "ffn":
            up_sums, *up_cut = ffn_back(
                table, tied(second_low, point), down_weight, mid_low, up_weight, up_bias
            )
            parts["U"] = Sum("U", up_cut[0], up_cut[1], ranks)
            parts["V"] = Sum("V", up_cut[2], up_cut[3], ranks)
            up_partial = up_cut[4:]
            up_got = [swap_cores(piece) for piece in up_partial]
            point = up_cut[0]
        elif item == "mid":
            first_grad, first_low, context_grad, mid_sums = mid(
                tied(second_grad, point), up_partial, up_got, mid_normal, mid_scale, mid_gain, out_weight
            )
            point = context_grad
        elif item == "back":
            grads, back_sums = attend_back(
                lengths, query, keys, values, log_total, tied(context_grad, point)
            )
            point = grads
        elif item == "cut":
            rest_cut = rest(
                table, tokens, context, tied(grads, point), first_low, last_sums, up_sums, mid_sums, back_sums
            )
            parts["R"] = Sum("R", rest_cut[0], rest_cut[1], ranks)
            parts["S"] = Sum("S", rest_cut[2], rest_cut[3], ranks)
            point = rest_cut[0]
        elif item == "tail":
            partial = input_part(tied(grads, point), query_weight, key_weight, value_weight)
            partial_got = swap_cores(partial)
            point = partial
        elif item == "fin":
            input_grad = (first_grad + (tied(partial, point) + partial_got)).astype(jnp.bfloat16)
            point = input_grad
        elif item == "vec":
            small = tied(parts["S"].extra, point).reshape(2, SUMS, BLOCK)
            small = jnp.concatenate([small[0], small[1]], axis=1)
            down_bias_grad, final_gain_grad, final_shift_grad = small[0], small[1], small[2]
            up_bias_grad = small[3 : 3 + hidden // width].reshape(-1)
            out_bias_grad, mid_gain_grad, mid_shift_grad = small[5], small[6], small[7]
            query_bias_grad, value_bias_grad = small[8, :columns], small[8, columns : 2 * columns]
            point = value_bias_grad
        elif item[1] == "j":
            family = {"E": "D", "V": "U", "S": "R"}.get(item[0], item[0])
            shapes = {
                "D": [(hidden, width)],
                "U": [(width, hidden)],
                "R": [(width, columns)] * 3 + [(columns, width)],
            }[family]
            place = list(PLAN).index(item[0]) * TABLE + 16
            part = parts[item[0]]
            joined[family] = join(
                item[0], table[place : place + 17], tied(part.own, point), part.got[7], shapes,
                joined.get(family, ()),
            )
            point = joined[family][0]
        else:
            point = parts[item[0]].step(int(item[1]), point)
    (down_weight_grad,), (up_weight_grad,) = joined["D"], joined["U"]
    query_weight_grad, key_weight_grad, value_weight_grad, out_weight_grad = joined["R"]
    return (
        layer_out,
        input_grad,
        query_weight_grad,
        query_bias_grad,
        key_weight_grad,
        value_weight_grad,
        value_bias_grad,
        out_weight_grad,
        out_bias_grad,
        mid_gain_grad,
        mid_shift_grad,
        up_weight_grad,
        up_bias_grad,
        down_weight_grad,
        down_bias_grad,
        final_gain_grad,
        final_shift_grad,
    )


def solution(mesh):
    rows, whole, split, vector = P("dp", None), P(), P(None, "mp"), P("mp")
    across = P("mp", None)
    in_specs = (
        rows, P("dp"), rows, split, vector, split, split, vector, across, whole, whole, whole,
        split, vector, across, whole, whole, whole,
    )
    out_specs = (
        rows, rows, split, vector, split, split, vector, across, whole, whole, whole,
        split, vector, across, whole, whole, whole,
    )
    ranks = mesh.shape["dp"]
    return jax.shard_map(
        functools.partial(body, ranks, device_tables(ranks)),
        mesh=mesh, in_specs=in_specs, out_specs=out_specs, check_vma=False,
    )
```

```python
import functools

import jax
import jax.numpy as jnp
import numpy as np
from jax import lax
from jax.experimental import pallas as pl
from jax.experimental.pallas import tpu as pltpu
from jax.sharding import PartitionSpec as P

DH = 64
BLOCK = 384
ROWS = {"D": (0, 192), "E": (192, 192), "U": (0, 176), "V": (176, 208), "R": (0, 176), "S": (176, 208)}
CUBE = 16
MIB = 1 << 20

norm_eps = 1e-12
score_scale = 0.125
root_half = 0.7071067811865476
inv_root_two_pi = 0.3989422804014327

PLAN = {"D": "Q", "E": "P", "U": "P", "V": "P", "R": "S", "S": "P"}
ORDER = (
    ("D1", "E1", "keep", "ffn", "V1", "mid", "back", "tail", "E2", "D2", "V2", "cut", "S1", "U1", "E3", "V3"),
    ("R1", "E4", "D3", "V4", "E5", "R2", "E6", "D4", "V5", "S2", "R3", "U2", "R4", "D5", "V6", "S3"),
    ("U3", "E7", "R5", "V7", "S4", "R6", "U4", "D6", "S5", "Vj", "fin", "R7", "U5", "S6", "D7", "Ej"),
    ("U6", "S7", "Rj", "U7", "Sj", "Dj", "vec", "Uj"),
)
ROUTES = {
    "P": ((1, 2), (2, 1), (4, 4)),
    "S": ((1, 2), (4, 4), (2, 1)),
    "Q": ((4, 4), (1, 2), (2, 1)),
}
ACROSS = (12, 12)


def coordinate(rank, mask):
    if mask == 1:
        return rank & 1
    if mask == 2:
        return (rank >> 1) & 1
    return ((rank >> 2) ^ (rank >> 3)) & 1


def block_places(name):
    sub = ROWS[name][0]
    places = []
    for block in range(8):
        high, low = block >> 1, block & 1
        if name in "DE":
            row, column = high * BLOCK + sub, low * BLOCK
            places.append((0, row, column, row, column))
        elif name in "UV":
            row, column = low * BLOCK + sub, high * BLOCK
            places.append((0, row, column, row, column))
        elif high < 3:
            row = low * BLOCK + sub
            places.append((high, row, 0, row, high * BLOCK))
        else:
            places.append((3, sub, low * BLOCK, 2 * BLOCK + sub, (3 + low) * BLOCK))
    return places


def device_tables(ranks):
    rows = []
    for rank in range(ranks):
        for core in range(2):
            row = []
            for name, route in PLAN.items():
                first, second, third = [coordinate(rank, pair[core]) for pair in ROUTES[route]]
                mine = 4 * first + 2 * second + third
                places = block_places(name)
                row += [places[spot ^ mine][3] for spot in range(8)]
                row += [places[spot ^ mine][4] for spot in range(8)]
                near = [(block ^ mine) & 3 for block in range(8)]
                far = list(near)
                for block in range(8):
                    edge = 4 if block < 4 else 3
                    if block >> 2 == first:
                        far[block] = near[edge]
                    else:
                        near[block] = (edge ^ mine) & 3
                row += near + far + [first]
            rows.append(row)
    return np.array(rows, np.int32)


TABLE = 33
PIECES = 4


def matmul(left, right):
    return jnp.dot(left, right, preferred_element_type=jnp.float32)


def matmul_flip(left, right):
    return lax.dot_general(
        left, right, (((1,), (1,)), ((), ())), preferred_element_type=jnp.float32
    )


def outer_sum(left, right):
    return lax.dot_general(
        left, right, (((0,), (0,)), ((), ())), preferred_element_type=jnp.float32
    )


def wide(ref):
    return ref[...].astype(jnp.float32)


def across(ref):
    return wide(ref).reshape(1, -1)


def row_mean(value):
    return jnp.mean(value, axis=-1, keepdims=True)


def norm_parts(value):
    center = value - row_mean(value)
    scale = lax.rsqrt(row_mean(center * center) + norm_eps)
    return center * scale, scale


def norm_lower(along, normal, scale):
    return scale * (along - row_mean(along) - normal * row_mean(along * normal))


def column_sum(value):
    return jnp.sum(value, axis=0, keepdims=True)


def cost(flops, bytes_accessed, transcendentals=0):
    return pl.CostEstimate(flops=1, bytes_accessed=1, transcendentals=0)


def call(kernel, ins, outs, estimate, limit, scalars=1, scratch=()):
    specs = [
        pl.BlockSpec(memory_space=pltpu.SMEM if place < scalars else pltpu.VMEM)
        for place in range(len(ins))
    ]
    return pl.pallas_call(
        kernel,
        out_shape=tuple(jax.ShapeDtypeStruct(shape, kind) for shape, kind in outs),
        in_specs=specs,
        out_specs=tuple(pl.BlockSpec(memory_space=pltpu.VMEM) for _ in outs),
        scratch_shapes=list(scratch),
        compiler_params=pltpu.CompilerParams(vmem_limit_bytes=limit * MIB),
        cost_estimate=estimate,
    )(*ins)


class Arrival:
    def __init__(self, source, target, sem):
        self.target = target
        self.copy = pltpu.make_async_copy(source, target, sem)
        self.copy.start()
        self.here = False
        self.shape = target.shape

    def wait(self):
        if not self.here:
            self.copy.wait()
            self.here = True

    def __getitem__(self, place):
        self.wait()
        return self.target[place]


class Departure:
    def __init__(self, source, target, sem):
        self.source = source
        self.copy = pltpu.make_async_copy(source, target, sem)
        self.shape = source.shape

    def __getitem__(self, place):
        return self.source[place]

    def __setitem__(self, place, value):
        self.source[place] = value

    def send(self):
        self.copy.start()


def mixed(kernel, ins, far_ins, outs, far_outs, estimate, limit, scalars=0, scratch=()):
    far_in = [pltpu.with_memory_space_constraint(array, pltpu.HBM) for array in far_ins]
    near_count, far_count, near_outs = len(ins), len(far_ins), len(outs)

    def body(*refs):
        near, refs = refs[:near_count], refs[near_count:]
        sources, refs = refs[:far_count], refs[far_count:]
        results, refs = refs[:near_outs], refs[near_outs:]
        targets, refs = refs[: len(far_outs)], refs[len(far_outs) :]
        held, refs = refs[:far_count], refs[far_count:]
        kept, refs = refs[: len(far_outs)], refs[len(far_outs) :]
        in_sem, out_sem = refs[:2]
        arrivals = [Arrival(sources[k], held[k], in_sem.at[k]) for k in range(far_count)]
        departures = [Departure(kept[k], targets[k], out_sem.at[k]) for k in range(len(far_outs))]
        kernel(*near, *arrivals, *results, *departures, *refs[2:])
        for departure in departures:
            departure.copy.wait()

    far, close = pl.BlockSpec(memory_space=pltpu.HBM), pl.BlockSpec(memory_space=pltpu.VMEM)
    small = pl.BlockSpec(memory_space=pltpu.SMEM)
    return pl.pallas_call(
        body,
        out_shape=tuple(jax.ShapeDtypeStruct(shape, kind) for shape, kind in outs)
        + tuple(pltpu.HBM(shape, kind) for shape, kind in far_outs),
        in_specs=[small] * scalars + [close] * (near_count - scalars) + [far] * far_count,
        out_specs=tuple([close] * near_outs + [far] * len(far_outs)),
        scratch_shapes=[pltpu.VMEM(array.shape, array.dtype) for array in far_ins]
        + [pltpu.VMEM(shape, kind) for shape, kind in far_outs]
        + [pltpu.SemaphoreType.DMA((max(1, far_count),)), pltpu.SemaphoreType.DMA((max(1, len(far_outs)),))]
        + list(scratch),
        compiler_params=pltpu.CompilerParams(vmem_limit_bytes=limit * MIB),
        cost_estimate=estimate,
    )(*ins, *far_in)


def head_of(lanes, head):
    return (lanes // DH) == head


def scores_flip(keys, query, limit):
    scores = matmul_flip(keys, query)
    visible = lax.broadcasted_iota(jnp.int32, scores.shape, 0) < limit
    return jnp.where(visible, scores, -1e30)


def attend_kernel(
    lengths, inputs, query_weight, query_bias, key_weight, value_weight, value_bias, out_weight, out_bias,
    partial_ref, query_ref, keys_ref, values_ref, context_ref, log_ref,
):
    query_ref[...] = (matmul(inputs[...], query_weight[...]) + across(query_bias)).astype(jnp.bfloat16)
    query_ref.send()
    keys_ref[...] = matmul(inputs[...], key_weight[...]).astype(jnp.bfloat16)
    keys_ref.send()
    values_ref[...] = (matmul(inputs[...], value_weight[...]) + across(value_bias)).astype(jnp.bfloat16)
    values_ref.send()
    limit = lengths[0]
    for pair in range(query_ref.shape[1] // (2 * DH)):
        columns = slice(pair * 2 * DH, (pair + 1) * 2 * DH)
        query = query_ref[:, columns] * jnp.bfloat16(score_scale)
        keys = keys_ref[:, columns]
        values = values_ref[:, columns]
        lanes = lax.broadcasted_iota(jnp.int32, query.shape, 1)
        sides = []
        for head in range(2):
            scores = scores_flip(keys, jnp.where(head_of(lanes, head), query, 0), limit)
            top = jnp.max(scores, axis=0, keepdims=True)
            raised = jnp.exp(scores - top)
            total = jnp.sum(raised, axis=0, keepdims=True)
            chances = (raised * (1.0 / total)).astype(jnp.bfloat16)
            log_ref[2 * pair + head : 2 * pair + head + 1, :] = top + jnp.log(total)
            sides.append(outer_sum(values, chances))
        rows = lax.broadcasted_iota(jnp.int32, sides[0].shape, 0)
        context = jnp.where(head_of(rows, 0), sides[0], sides[1])
        context_ref[:, columns] = context.T.astype(jnp.bfloat16)
    context_ref.send()
    log_ref.send()
    partial_ref[...] = matmul(context_ref[...], out_weight[...]) + 0.5 * across(out_bias)


def attend(
    lengths, tokens, query_weight, query_bias, key_weight, value_weight, value_bias, out_weight, out_bias
):
    rows, width = tokens.shape
    columns = query_weight.shape[1]
    partial, query, keys, values, context, log_total = mixed(
        attend_kernel,
        (lengths,),
        (tokens, query_weight, query_bias, key_weight, value_weight, value_bias, out_weight, out_bias),
        (((rows, width), jnp.float32),),
        [((rows, columns), jnp.bfloat16)] * 4 + [((8, rows), jnp.float32)],
        cost(8 * rows * width * columns + 8 * rows * rows * columns, 8 * MIB),
        limit=20,
        scalars=1,
    )
    return query, keys, values, context, log_total, partial


def phi(before):
    return 0.5 * (1.0 + lax.erf(before * root_half))


def ffn_kernel(
    tokens, own, got, up_weight, mid_gain, mid_shift, up_bias, down_weight, down_bias,
    partial_ref, middle_ref, normal_ref, scale_ref, low_ref, flipped_ref, active,
):
    normal, scale = norm_parts(wide(tokens) + (own[...] + got[...]))
    middle = normal * across(mid_gain) + across(mid_shift)
    middle_ref[...] = middle
    middle_ref.send()
    low_ref[...] = middle.astype(jnp.bfloat16)
    low_ref.send()
    normal_ref[...] = normal
    normal_ref.send()
    scale_ref[...] = scale
    scale_ref.send()
    hidden = up_weight.shape[1]
    bias = across(up_bias)
    for start in range(0, hidden, 256):
        columns = slice(start, start + 256)
        before = matmul(low_ref[...], up_weight[:, columns]) + bias[:, columns]
        active[:, columns] = (before * phi(before)).astype(jnp.bfloat16)
    flip_into(flipped_ref, active)
    flipped_ref.send()
    partial_ref[...] = matmul(active[...], down_weight[...]) + 0.5 * across(down_bias)


def ffn(tokens, own, got, mid_gain, mid_shift, up_weight, up_bias, down_weight, down_bias):
    rows, width = tokens.shape
    hidden = up_weight.shape[1]
    full = ((rows, width), jnp.float32)
    return mixed(
        ffn_kernel,
        (tokens, own, got, up_weight),
        (mid_gain, mid_shift, up_bias, down_weight, down_bias),
        (full,),
        (full, full, ((rows, 1), jnp.float32), ((rows, width), jnp.bfloat16), ((hidden, rows), jnp.bfloat16)),
        cost(4 * rows * width * hidden, 16 * MIB, rows * hidden),
        limit=26,
        scratch=[pltpu.VMEM((rows, hidden), jnp.bfloat16)],
    )


def cut(offsets, flipped, right, targets, first, spots):
    for part in range(2):
        base = (first + part) * TABLE
        rows = ROWS["DEUVRS"[first + part]][1]
        for place, spot in enumerate(spots):
            row = pl.multiple_of(offsets[base + spot], 16)
            column = pl.multiple_of(offsets[base + 8 + spot], 128)
            targets[part][place * rows : (place + 1) * rows, :] = matmul(
                flipped[pl.ds(row, rows), :], right[:, pl.ds(column, BLOCK)]
            )


KEPT = (0, 1, 2, 3)
SENT = (4, 5, 6, 7)


def flip_into(flipped, left, start=0):
    for column in range(0, left.shape[1], 128):
        flipped[start + column : start + column + 128, :] = left[:, column : column + 128].T


SUMS = 16


def blocks(name, more=0):
    return ((4 * ROWS[name][1] + more, BLOCK), jnp.float32)


def sums(width):
    return ((8, width), jnp.float32)


def last_kernel(
    offsets, middle, own, got, cotangent, final_gain, flipped,
    second_ref, low_ref, final_ref, send0, send1,
):
    final, scale = norm_parts(middle[...] + (own[...] + got[...]))
    final_ref[...] = final
    second = norm_lower(wide(cotangent) * across(final_gain), final, scale)
    low_ref[...] = second.astype(jnp.bfloat16)
    second_ref[...] = second
    flipped.wait()
    cut(offsets, flipped.target, low_ref, (send0, send1), 0, SENT)


def last(offsets, middle, own, got, cotangent, final_gain, flipped):
    rows, width = middle.shape
    full = ((rows, width), jnp.float32)
    return mixed(
        last_kernel,
        (offsets, middle, own, got),
        (cotangent, final_gain, flipped),
        (full, ((rows, width), jnp.bfloat16), full, blocks("D"), blocks("E")),
        (),
        cost(rows * width * flipped.shape[0], 14 * MIB),
        limit=24,
        scalars=1,
    )


def keep_kernel(
    offsets, second, low, final, final_gain, final_shift, cotangent, flipped, out_ref, sums_ref, keep0, keep1
):
    cut(offsets, flipped, low, (keep0, keep1), 0, KEPT)
    upper = wide(cotangent)
    sums_ref[...] = jnp.zeros_like(sums_ref)
    sums_ref[0:1, :] = column_sum(second[...])
    sums_ref[1:2, :] = column_sum(upper * final[...])
    sums_ref[2:3, :] = column_sum(upper)
    out_ref[...] = (final[...] * across(final_gain) + across(final_shift)).astype(jnp.bfloat16)


def keep(offsets, second, low, final, final_gain, final_shift, cotangent, flipped):
    rows, width = low.shape
    return call(
        keep_kernel,
        (offsets, second, low, final, final_gain, final_shift, cotangent, flipped),
        (((rows, width), jnp.bfloat16), sums(width), blocks("D"), blocks("E")),
        cost(rows * width * flipped.shape[0], 14 * MIB),
        limit=26,
    )


def ffn_back_kernel(
    offsets, second_low, down_weight, low, up_weight, up_bias,
    sums_ref, send0, keep0, send1, keep1, *rest,
):
    partial_refs, before_grad, flipped = rest[:PIECES], rest[-2], rest[-1]
    hidden = up_weight.shape[1]
    width = sums_ref.shape[1]
    bias = across(up_bias)
    sums_ref[...] = jnp.zeros_like(sums_ref)
    for start in range(0, hidden, 256):
        columns = slice(start, start + 256)
        before = matmul(low[...], up_weight[:, columns]) + bias[:, columns]
        slope = phi(before) + before * inv_root_two_pi * jnp.exp(-0.5 * before * before)
        grad = (matmul_flip(second_low[...], down_weight[columns, :]) * slope).astype(jnp.bfloat16)
        before_grad[:, columns] = grad
        row, place = start // width, start % width
        sums_ref[row : row + 1, place : place + 256] = column_sum(grad.astype(jnp.float32))
    for place, partial_ref in enumerate(partial_refs):
        rows = slice(place * partial_ref.shape[0], (place + 1) * partial_ref.shape[0])
        partial_ref[...] = matmul_flip(before_grad[rows, :], up_weight[...])
    flip_into(flipped, low)
    cut(offsets, flipped, before_grad, (send0, send1), 2, SENT)
    cut(offsets, flipped, before_grad, (keep0, keep1), 2, KEPT)


def ffn_back(offsets, second_low, down_weight, low, up_weight, up_bias):
    rows, width = low.shape
    hidden = up_weight.shape[1]
    return call(
        ffn_back_kernel,
        (offsets, second_low, down_weight, low, up_weight, up_bias),
        (sums(width), blocks("U"), blocks("U"), blocks("V"), blocks("V")) + (((rows // PIECES, width), jnp.float32),) * PIECES,
        cost(6 * rows * width * hidden, 18 * MIB, 2 * rows * hidden),
        scratch=[pltpu.VMEM((rows, hidden), jnp.bfloat16), pltpu.VMEM((width, rows), jnp.bfloat16)],
        limit=26,
    )


def mid_kernel(second, normal_ref, scale, mid_gain, out_weight, *rest):
    own, got = rest[:PIECES], rest[PIECES : 2 * PIECES]
    first_ref, low_ref, context_grad, sums_ref, upper = rest[2 * PIECES :]
    for place in range(PIECES):
        rows = slice(place * own[place].shape[0], (place + 1) * own[place].shape[0])
        upper[rows, :] = second[rows, :] + (own[place][...] + got[place][...])
    normal = normal_ref[...]
    sums_ref[...] = jnp.zeros_like(sums_ref)
    sums_ref[1:2, :] = column_sum(upper[...] * normal)
    sums_ref[2:3, :] = column_sum(upper[...])
    first = norm_lower(upper[...] * across(mid_gain), normal, scale[...])
    sums_ref[0:1, :] = column_sum(first)
    first_ref[...] = first
    low_ref[...] = first.astype(jnp.bfloat16)
    context_grad[...] = matmul_flip(low_ref[...], out_weight[...]).astype(jnp.bfloat16)


def mid(second, own, got, normal, scale, mid_gain, out_weight):
    rows, width = second.shape
    columns = out_weight.shape[0]
    return call(
        mid_kernel,
        (second, normal, scale, mid_gain, out_weight, *own, *got),
        (
            ((rows, width), jnp.float32),
            ((rows, width), jnp.bfloat16),
            ((rows, columns), jnp.bfloat16),
            sums(width),
        ),
        cost(2 * rows * width * columns, 10 * MIB),
        scalars=0,
        scratch=[pltpu.VMEM((rows, width), jnp.float32)],
        limit=20,
    )


def attend_back_kernel(
    lengths, query_ref, keys_ref, values_ref, log_ref, upstream_ref,
    grads_ref, sums_ref,
):
    limit = lengths[0]
    sums_ref[...] = jnp.zeros_like(sums_ref)
    width = query_ref.shape[1]
    @pl.loop(0, width // (2 * DH))
    def _(pair):
        start = pl.multiple_of(pair * 2 * DH, 2 * DH)
        columns = pl.ds(start, 2 * DH)
        query = query_ref[:, columns] * jnp.bfloat16(score_scale)
        keys = keys_ref[:, columns]
        values = values_ref[:, columns]
        upstream = upstream_ref[:, columns]
        lanes = lax.broadcasted_iota(jnp.int32, query.shape, 1)
        value_grad = jnp.zeros(query.shape, jnp.float32)
        key_grad = jnp.zeros(query.shape, jnp.float32)
        sides = []
        for head in range(2):
            mine = head_of(lanes, head)
            asked = jnp.where(mine, query, 0)
            pulled = jnp.where(mine, upstream, 0)
            scores = scores_flip(keys, asked, limit)
            chances = jnp.exp(scores - log_ref[pl.ds(2 * pair + head, 1), :])
            value_grad = value_grad + matmul(chances.astype(jnp.bfloat16), pulled)
            spread = matmul_flip(values, pulled).astype(jnp.bfloat16).astype(jnp.float32)
            common = jnp.sum(spread * chances, axis=0, keepdims=True)
            score_grad = (chances * (spread - common)).astype(jnp.bfloat16)
            key_grad = key_grad + matmul(score_grad, asked)
            sides.append(outer_sum(keys, score_grad))
        rows = lax.broadcasted_iota(jnp.int32, sides[0].shape, 0)
        query_grad = (jnp.where(head_of(rows, 0), sides[0], sides[1]).T * score_scale).astype(jnp.bfloat16)
        key_low = key_grad.astype(jnp.bfloat16)
        value_low = value_grad.astype(jnp.bfloat16)
        grads_ref[:, columns] = query_grad
        grads_ref[:, pl.ds(width + start, 2 * DH)] = key_low
        grads_ref[:, pl.ds(2 * width + start, 2 * DH)] = value_low
        sums_ref[0:1, columns] = column_sum(query_grad.astype(jnp.float32))
        sums_ref[0:1, pl.ds(width + start, 2 * DH)] = column_sum(
            value_low.astype(jnp.float32)
        )


def attend_back(lengths, query, keys, values, log_total, upstream):
    rows, width = query.shape
    return call(
        attend_back_kernel,
        (lengths, query, keys, values, log_total, upstream),
        (((rows, 3 * width), jnp.bfloat16), sums(2 * width)),
        cost(20 * rows * rows * width, 4 * MIB, rows * rows * width // DH),
        limit=16,
    )


def rest_kernel(
    offsets, tokens, context, grads, first_low, last_sums, up_sums, mid_sums, back_sums,
    send0, keep0, send1, keep1, flipped, right,
):
    flip_into(flipped, tokens)
    flip_into(flipped, context, tokens.shape[1])
    right[:, : grads.shape[1]] = grads[...]
    right[:, grads.shape[1] :] = first_low[...]
    cut(offsets, flipped, right, (send0, send1), 4, SENT)
    cut(offsets, flipped, right, (keep0, keep1), 4, KEPT)
    rows = [last_sums[0:3, :], up_sums[0:2, :], mid_sums[0:3, :], back_sums[0:1, :]]
    end = send1.shape[0] - 2 * SUMS
    send1[end:, :] = jnp.zeros((2 * SUMS, BLOCK), jnp.float32)
    for half in range(2):
        place = end + half * SUMS
        for part in rows:
            send1[place : place + part.shape[0], :] = part[:, half * BLOCK : (half + 1) * BLOCK]
            place = place + part.shape[0]


def rest(offsets, tokens, context, grads, first_low, last_sums, up_sums, mid_sums, back_sums):
    rows, width = tokens.shape
    left = width + context.shape[1]
    right = grads.shape[1] + width
    return call(
        rest_kernel,
        (offsets, tokens, context, grads, first_low, last_sums, up_sums, mid_sums, back_sums),
        (blocks("R"), blocks("R"), blocks("S", 2 * SUMS), blocks("S")),
        cost(16 * rows * BLOCK * BLOCK, 8 * MIB),
        scratch=[pltpu.VMEM((left, rows), jnp.bfloat16), pltpu.VMEM((rows, right), jnp.bfloat16)],
        limit=16,
    )


def input_kernel(grads, query_weight, key_weight, value_weight, partial_ref):
    width = query_weight.shape[1]
    partial_ref[...] = (
        matmul_flip(grads[:, :width], query_weight[...])
        + matmul_flip(grads[:, width : 2 * width], key_weight[...])
        + matmul_flip(grads[:, 2 * width :], value_weight[...])
    )


def input_part(grads, query_weight, key_weight, value_weight):
    rows, width = grads.shape[0], query_weight.shape[0]
    return call(
        input_kernel,
        (grads, query_weight, key_weight, value_weight),
        (((rows, width), jnp.float32),),
        cost(2 * rows * width * grads.shape[1], 6 * MIB),
        scalars=0,
        limit=10,
    )[0]


def join_kernel(name, table, near, far, *rest):
    places = block_places(name)
    rows = ROWS[name][1]
    count = len({place[0] for place in places})
    outs, done = rest[-count - 1 : -1], rest[-1]
    for side in range(2):

        @pl.when(table[16] == side)
        def _():
            copies = []
            for block in range(8):
                out, row, column = places[block][:3]
                source = near if block >> 2 == side else far
                copies.append(
                    pltpu.make_async_copy(
                        source.at[pl.ds(pl.multiple_of(table[8 * (source is far) + block] * rows, 8), rows)],
                        outs[out].at[pl.ds(row, rows), pl.ds(column, BLOCK)],
                        done.at[block],
                    )
                )
            for copy in copies:
                copy.start()
            for copy in copies:
                copy.wait()


def join(name, table, near, far, shapes, earlier):
    specs = [
        pl.BlockSpec(memory_space=pltpu.SMEM),
        pl.BlockSpec(memory_space=pltpu.VMEM),
        pl.BlockSpec(memory_space=pltpu.VMEM),
    ] + [pl.BlockSpec(memory_space=pl.ANY) for _ in earlier]
    return pl.pallas_call(
        functools.partial(join_kernel, name),
        out_shape=tuple(jax.ShapeDtypeStruct(shape, jnp.float32) for shape in shapes),
        in_specs=specs,
        out_specs=tuple(pl.BlockSpec(memory_space=pl.ANY) for _ in shapes),
        scratch_shapes=[pltpu.SemaphoreType.DMA((8,))],
        input_output_aliases={3 + place: place for place in range(len(earlier))},
        compiler_params=pltpu.CompilerParams(vmem_limit_bytes=16 * MIB),
        cost_estimate=cost(0, 8 * near.size),
    )(table, near, far, *earlier)


def swap_cores(part):
    return lax.ppermute(part, "mp", [(0, 1), (1, 0)])


def hop(block, masks, ranks):
    pairs = [
        (2 * rank + core, 2 * (rank ^ masks[core]) + core) for rank in range(ranks) for core in (0, 1)
    ]
    return lax.ppermute(block, ("dp", "mp"), pairs)


def tied(value, before):
    return value if before is None else lax.optimization_barrier((value, before))[0]


class Sum:
    def __init__(self, name, send, keep, ranks):
        self.name, self.send, self.keep, self.ranks = name, send, keep, ranks
        self.masks = ROUTES[PLAN[name]] + (ACROSS,)
        self.got = {}
        self.rows = ROWS[name][1]
        self.extra = send[4 * self.rows :] if send.shape[0] > 4 * self.rows else None

    def with_extra(self, value, got, rows):
        if self.extra is None:
            return value
        self.extra = self.extra + got[rows:]
        return jnp.concatenate([value, self.extra])

    def step(self, number, before):
        got, one, two = self.got, self.rows, 2 * self.rows
        keep = tied(self.own if number > 4 else self.keep if number > 1 else self.send, before)
        if number == 1:
            value = keep
        elif number == 2:
            value = self.with_extra(keep[two:] + got[1][two : 2 * two], got[1], 2 * two)
        elif number == 3:
            value = self.with_extra(keep[one:two] + got[1][one:two] + got[2][one:two], got[2], two)
        elif number == 4:
            value = keep[:one] + got[1][:one] + got[2][:one] + got[3][:one]
            value = self.with_extra(value, got[3], one)
        elif number == 5:
            value = keep + got[4]
            bit = CUBE
            while bit < self.ranks:
                value = value + hop(value, (bit, bit), self.ranks)
                bit = 2 * bit
            if self.extra is not None:
                value, self.extra = value[:one], value[one:]
        elif number == 6:
            value = jnp.concatenate([keep, got[5]])
        else:
            value = jnp.concatenate([keep, got[6]])
        self.own = value
        with jax.named_scope(f"{self.name}{number}"):
            got[number] = hop(value, self.masks[min(number, 8 - number) - 1], self.ranks)
        return value


def body(
    ranks,
    tables,
    tokens,
    lengths,
    cotangent,
    query_weight,
    query_bias,
    key_weight,
    value_weight,
    value_bias,
    out_weight,
    out_bias,
    mid_gain,
    mid_shift,
    up_weight,
    up_bias,
    down_weight,
    down_bias,
    final_gain,
    final_shift,
):
    table = jnp.asarray(tables)[2 * lax.axis_index("dp") + lax.axis_index("mp")]
    width = tokens.shape[1]
    columns = query_weight.shape[1]
    hidden = up_weight.shape[1]

    query, keys, values, context, log_total, partial = attend(
        lengths, tokens, query_weight, query_bias, key_weight, value_weight, value_bias, out_weight, out_bias
    )
    down_partial, middle, mid_normal, mid_scale, mid_low, active_flip = ffn(
        tokens, partial, swap_cores(partial), mid_gain, mid_shift, up_weight, up_bias, down_weight, down_bias
    )
    second_grad, second_low, final_normal, *down_sent = last(
        table, middle, down_partial, swap_cores(down_partial), cotangent, final_gain, active_flip
    )
    parts = {
        "D": Sum("D", down_sent[0], None, ranks),
        "E": Sum("E", down_sent[1], None, ranks),
    }
    point = None
    joined = {}
    for item in sum(ORDER, ()):
        if item == "keep":
            layer_out, last_sums, *down_kept = keep(
                table, second_grad, tied(second_low, point), final_normal, final_gain, final_shift,
                cotangent, active_flip,
            )
            parts["D"].keep, parts["E"].keep = down_kept
            point = down_kept[0]
        elif item == "ffn":
            up_sums, *up_cut = ffn_back(
                table, tied(second_low, point), down_weight, mid_low, up_weight, up_bias
            )
            parts["U"] = Sum("U", up_cut[0], up_cut[1], ranks)
            parts["V"] = Sum("V", up_cut[2], up_cut[3], ranks)
            up_partial = up_cut[4:]
            up_got = [swap_cores(piece) for piece in up_partial]
            point = up_cut[0]
        elif item == "mid":
            first_grad, first_low, context_grad, mid_sums = mid(
                tied(second_grad, point), up_partial, up_got, mid_normal, mid_scale, mid_gain, out_weight
            )
            point = context_grad
        elif item == "back":
            grads, back_sums = attend_back(
                lengths, query, keys, values, log_total, tied(context_grad, point)
            )
            point = grads
        elif item == "cut":
            rest_cut = rest(
                table, tokens, context, tied(grads, point), first_low, last_sums, up_sums, mid_sums, back_sums
            )
            parts["R"] = Sum("R", rest_cut[0], rest_cut[1], ranks)
            parts["S"] = Sum("S", rest_cut[2], rest_cut[3], ranks)
            point = rest_cut[0]
        elif item == "tail":
            partial = input_part(tied(grads, point), query_weight, key_weight, value_weight)
            partial_got = swap_cores(partial)
            point = partial
        elif item == "fin":
            input_grad = (first_grad + (tied(partial, point) + partial_got)).astype(jnp.bfloat16)
            point = input_grad
        elif item == "vec":
            small = tied(parts["S"].extra, point).reshape(2, SUMS, BLOCK)
            small = jnp.concatenate([small[0], small[1]], axis=1)
            down_bias_grad, final_gain_grad, final_shift_grad = small[0], small[1], small[2]
            up_bias_grad = small[3 : 3 + hidden // width].reshape(-1)
            out_bias_grad, mid_gain_grad, mid_shift_grad = small[5], small[6], small[7]
            query_bias_grad, value_bias_grad = small[8, :columns], small[8, columns : 2 * columns]
            point = value_bias_grad
        elif item[1] == "j":
            family = {"E": "D", "V": "U", "S": "R"}.get(item[0], item[0])
            shapes = {
                "D": [(hidden, width)],
                "U": [(width, hidden)],
                "R": [(width, columns)] * 3 + [(columns, width)],
            }[family]
            place = list(PLAN).index(item[0]) * TABLE + 16
            part = parts[item[0]]
            joined[family] = join(
                item[0], table[place : place + 17], tied(part.own, point), part.got[7], shapes,
                joined.get(family, ()),
            )
            point = joined[family][0]
        else:
            point = parts[item[0]].step(int(item[1]), point)
    (down_weight_grad,), (up_weight_grad,) = joined["D"], joined["U"]
    query_weight_grad, key_weight_grad, value_weight_grad, out_weight_grad = joined["R"]
    return (
        layer_out,
        input_grad,
        query_weight_grad,
        query_bias_grad,
        key_weight_grad,
        value_weight_grad,
        value_bias_grad,
        out_weight_grad,
        out_bias_grad,
        mid_gain_grad,
        mid_shift_grad,
        up_weight_grad,
        up_bias_grad,
        down_weight_grad,
        down_bias_grad,
        final_gain_grad,
        final_shift_grad,
    )


def solution(mesh):
    rows, whole, split, vector = P("dp", None), P(), P(None, "mp"), P("mp")
    across = P("mp", None)
    in_specs = (
        rows, P("dp"), rows, split, vector, split, split, vector, across, whole, whole, whole,
        split, vector, across, whole, whole, whole,
    )
    out_specs = (
        rows, rows, split, vector, split, split, vector, across, whole, whole, whole,
        split, vector, across, whole, whole, whole,
    )
    ranks = mesh.shape["dp"]
    return jax.shard_map(
        functools.partial(body, ranks, device_tables(ranks)),
        mesh=mesh, in_specs=in_specs, out_specs=out_specs, check_vma=False,
    )
```
